128 devices in a mesh: view: 4 (over y_hi, core), tile: 32 (over z, y_lo, x).
Axes of the slice: x: 4, y: 4 (y_hi: 2, y_lo: 2; y = y_hi * 2 + y_lo), z: 4, core: 2. Of those that a mesh axis runs over, the one named last changes fastest.
Arguments:
- objects: float32 [4, 2, 128, 1024], P('view', None, None, 'tile'), may hold values from -6 to 6
- probe: float32 [2, 128, 128], replicated, may hold values from -0.75 to 0.75
- positions: int32 [4, 256], P('view', 'tile'), may hold values from 0 to 896, as said below
- amplitudes: float32 [4, 256, 128, 128], P('view', 'tile'), may hold values from 0 to 0.53033006
- reproj_prev: float32 [4, 2, 128, 1024], P('view', None, None, 'tile'), may hold values from -6 to 6
- multipliers: float32 [4, 2, 128, 1024], P('view', None, None, 'tile'), may hold values from -4 to 4
- volume: float32 [2, 128, 1024, 1024], P(None, ('view', 'tile')), may hold values from -6 to 6
- angles: int32 [4], replicated, may hold values from 0 to 3
- penalty: int32 [2], replicated, may hold values from 1 to 5, as said below
Outputs:
- reprojections: float32 [4, 2, 128, 1024], P('view', None, None, 'tile')
- new_multipliers: float32 [4, 2, 128, 1024], P('view', None, None, 'tile')
The draws below stay inside these ranges and needn't reach their ends.
Inputs may be any that keep to these rules, and one draw needn't show every extreme that they name: `positions`: the window of a scan covers 128 columns inside the strip. The penalty is the first entry divided by the second; the first is 1 to 4, the second is 5. `angles`: angle index k is a view at k times 90 degrees.
All inputs are finite; a program needn't handle non-finite values.
Results may differ from the reference program's by a relative error of at most 0.0001.
Values sent between devices are 32-bit elements; how exact they have to be, the bound alone decides.
A program may use at most 64 MiB of HBM per device.

```python
import math
import jax
import jax.numpy as jnp
from jax import lax

N = 1024
PS = 128
SLICES = 128
ITERS = 2
VIEWS = 4
SCANS = 256
COVER = 32


def draw_positions(key, part):
    starts = jax.random.randint(key, (VIEWS, SCANS), 0, N - PS + 1)
    starts = starts.at[0, 0].set(0).at[0, 1].set(N - PS)
    return starts.astype(jnp.int32)


def draw_penalty(key, part):
    upper = jax.random.randint(jax.random.fold_in(key, 11), (1,), 1, 5)
    lower = jnp.full((1,), 5, jnp.int32)
    return jnp.concatenate([upper.astype(jnp.int32), lower]).astype(jnp.int32)


def place_ends(array, rng, low, high):
    longest = array.shape.index(max(array.shape))
    spots = []
    for shift in (0, 1):
        where = [jax.random.randint(jax.random.fold_in(rng, axis), (), 0, length) for axis, length in enumerate(array.shape)]
        where[longest] = (where[longest] + shift) % array.shape[longest]
        spots.append(tuple(where))
    return array.at[spots[0]].set(low).at[spots[1]].set(high)


def levels(key, extent, split, low, top_value):
    factor_of = 1.0
    for position, blocks in split:
        heights = jax.random.uniform(jax.random.fold_in(jax.random.fold_in(key, 6), position), (blocks,), jnp.float32, low / len(split), top_value / len(split))
        factor_of = factor_of * jnp.repeat(jnp.exp(heights), extent[position] // blocks).reshape((-1,) + (1,) * (len(extent) - 1 - position))
    return factor_of


def gaussian(key, extent, scale, limit, pieces=(), kind=jnp.bfloat16):
    values = jax.random.normal(key, extent, jnp.float32) * scale
    if len(pieces) > 0:
        values = levels(key, extent, pieces, -0.22, 0.18) * values
    return jnp.clip(values, min=-limit, max=limit).astype(kind)


def setup_inputs(seed: int = 0) -> dict:
    key_list = jax.random.split(jax.random.key(seed), 10)
    return {
        "objects": gaussian(key_list[0], (VIEWS, 2, SLICES, N), 1.0, 6.0, ((0, 4), (3, 32)), jnp.float32),
        "probe": gaussian(key_list[1], (2, SLICES, PS), (2 * COVER) ** -0.5, 0.75, (), jnp.float32),
        "positions": draw_positions(jax.random.fold_in(key_list[9], 71), 0),
        "amplitudes": jnp.clip(0.53033006 * jax.random.uniform(key_list[3], (VIEWS, SCANS, SLICES, PS), jnp.float32) ** levels(key_list[3], (VIEWS, SCANS, SLICES, PS), ((0, 4), (1, 32)), -0.2, 0.2), 0.0, 0.53033006),
        "reproj_prev": gaussian(key_list[4], (VIEWS, 2, SLICES, N), 1.0, 6.0, ((0, 4), (3, 32)), jnp.float32),
        "multipliers": gaussian(key_list[5], (VIEWS, 2, SLICES, N), 0.5, 4.0, ((0, 4), (3, 32)), jnp.float32),
        "volume": gaussian(key_list[6], (2, SLICES, N, N), 1.0, 6.0, ((1, 128),), jnp.float32),
        "angles": place_ends(jax.random.randint(key_list[7], (VIEWS,), 0, 4), jax.random.fold_in(key_list[7], 1), 0, 3).astype(jnp.int32),
        "penalty": draw_penalty(jax.random.fold_in(key_list[9], 71), 0),
    }


HIGHEST = lax.Precision.HIGHEST

def dft_tables(length):
    indices = jnp.arange(length, dtype=jnp.int32)
    phase = (indices[:, None] * indices[None, :] % length).astype(jnp.float32) * (2.0 * math.pi / length)
    factor = 1.0 / math.sqrt(length)
    return (jnp.cos(phase) * factor, -jnp.sin(phase) * factor)

def left_apply(cosine, sine, sign, real_part, imag_part):
    first = jnp.einsum('rk,nkc->nrc', cosine, real_part, precision=HIGHEST)
    second = jnp.einsum('rk,nkc->nrc', sine, imag_part, precision=HIGHEST)
    third = jnp.einsum('rk,nkc->nrc', cosine, imag_part, precision=HIGHEST)
    fourth = jnp.einsum('rk,nkc->nrc', sine, real_part, precision=HIGHEST)
    return (first - sign * second, third + sign * fourth)

def right_apply(cosine, sine, sign, real_part, imag_part):
    first = jnp.einsum('nrk,kc->nrc', real_part, cosine, precision=HIGHEST)
    second = jnp.einsum('nrk,kc->nrc', imag_part, sine, precision=HIGHEST)
    third = jnp.einsum('nrk,kc->nrc', imag_part, cosine, precision=HIGHEST)
    fourth = jnp.einsum('nrk,kc->nrc', real_part, sine, precision=HIGHEST)
    return (first - sign * second, third + sign * fourth)

def window_columns(starts, width):
    return (starts[:, None] + jnp.arange(width, dtype=jnp.int32)[None, :]).reshape(-1)

def strip_gradient(strip, starts, measured, probe, floor):
    rows = strip.shape[1]
    width = probe.shape[2]
    total = strip.shape[2]
    windows = jax.vmap(lambda start: lax.dynamic_slice_in_dim(strip, start, width, axis=2))(starts)
    window_re = windows[:, 0]
    window_im = windows[:, 1]
    probe_re = probe[0]
    probe_im = probe[1]
    exit_re = probe_re * window_re - probe_im * window_im
    exit_im = probe_re * window_im + probe_im * window_re
    row_cos, row_sin = dft_tables(rows)
    col_cos, col_sin = dft_tables(width)
    mid_re, mid_im = left_apply(row_cos, row_sin, 1.0, exit_re, exit_im)
    far_re, far_im = right_apply(col_cos, col_sin, 1.0, mid_re, mid_im)
    modulus = jnp.sqrt(far_re * far_re + far_im * far_im)
    keep = 1.0 - measured / jnp.maximum(modulus, floor)
    back_re, back_im = left_apply(row_cos, row_sin, -1.0, far_re * keep, far_im * keep)
    back_re, back_im = right_apply(col_cos, col_sin, -1.0, back_re, back_im)
    grad_re = probe_re * back_re + probe_im * back_im
    grad_im = probe_re * back_im - probe_im * back_re
    columns = window_columns(starts, width)
    values = jnp.stack([grad_re, grad_im], axis=0).transpose(0, 2, 1, 3).reshape(2, rows, -1)
    return jnp.zeros((2, rows, total), jnp.float32).at[:, :, columns].add(values)

def illumination(starts, probe, total):
    rows = probe.shape[1]
    width = probe.shape[2]
    power = probe[0] * probe[0] + probe[1] * probe[1]
    values = jnp.broadcast_to(power[:, None, :], (rows, starts.shape[0], width)).reshape(rows, -1)
    return jnp.zeros((rows, total), jnp.float32).at[:, window_columns(starts, width)].add(values)

def project(column_sum, row_sum, angles):
    length = column_sum.shape[-1]
    angle_grid = angles[:, None]
    along = column_sum[..., None, :]
    across = row_sum[..., None, :]
    result = jnp.where(angle_grid == 0, along, jnp.where(angle_grid == 1, across, jnp.where(angle_grid == 2, jnp.flip(along, -1), jnp.flip(across, -1))))
    return result * (1.0 / math.sqrt(length))

def backproject(lines, angles):
    length = lines.shape[-1]
    angle_grid = angles[:, None]
    zero = jnp.zeros_like(lines)
    column_term = lax.optimization_barrier(jnp.sum(jnp.where(angle_grid == 0, lines, zero), -2)) + jnp.flip(lax.optimization_barrier(jnp.sum(jnp.where(angle_grid == 2, lines, zero), -2)), -1)
    row_term = lax.optimization_barrier(jnp.sum(jnp.where(angle_grid == 1, lines, zero), -2)) + jnp.flip(lax.optimization_barrier(jnp.sum(jnp.where(angle_grid == 3, lines, zero), -2)), -1)
    return (column_term[..., None, :] + row_term[..., :, None]) * (1.0 / math.sqrt(length))

def reference(objects, probe, positions, amplitudes, reproj_prev, multipliers, volume, angles, penalty):
    penalty_value = penalty[0].astype(jnp.float32) / penalty[1].astype(jnp.float32)
    floor = 0.25 / math.sqrt(COVER)

    def one_view(inputs):
        strip, starts, measured, previous, lagrange = inputs
        power = illumination(starts, probe, strip.shape[2])
        for sweep in range(ITERS):
            grad = strip_gradient(strip, starts, measured, probe, floor)
            strip = strip - (grad + penalty_value * (strip - previous) + lagrange) / (power + penalty_value)
        return strip
    psi = lax.map(one_view, (objects, positions, amplitudes, reproj_prev, multipliers))
    views = objects.shape[0]

    def one_slice(index):
        slab = lax.dynamic_index_in_dim(volume, index, 1, keepdims=False)
        lines = jnp.transpose(lax.dynamic_index_in_dim(psi, index, 2, keepdims=False), (1, 0, 2))
        lagrange = jnp.transpose(lax.dynamic_index_in_dim(multipliers, index, 2, keepdims=False), (1, 0, 2))
        projected = project(slab.sum(1), slab.sum(2), angles)
        misfit = projected - lines - lagrange / penalty_value
        updated = slab - backproject(misfit, angles) / views
        fresh = project(updated.sum(1), updated.sum(2), angles)
        return (fresh, lagrange + penalty_value * (lines - fresh))
    fresh, lagrange = lax.map(one_slice, jnp.arange(SLICES, dtype=jnp.int32))
    return (jnp.transpose(fresh, (2, 1, 0, 3)), jnp.transpose(lagrange, (2, 1, 0, 3)))
```

```python
import math

import jax
import jax.numpy as jnp
import ml_dtypes
import numpy as np
from jax import lax
from jax.experimental import pallas as pl
from jax.experimental.pallas import tpu as pltpu
from jax.sharding import PartitionSpec as P

ITERS = 2
F32 = jnp.float32
BF16 = jnp.bfloat16
MESH = pl.DeviceIdType.MESH

ROWS = 128
TOTAL = 1024
SCANS = 8
TILE = 32
FLOOR = 0.25 / math.sqrt(SCANS * 32 * ROWS // TOTAL)

PEERS = sorted(
    [(dz, dx) for dz in range(4) for dx in range(4) if (dz, dx) != (0, 0)],
    key=lambda p: -(min(p[0], 4 - p[0]) + min(p[1], 4 - p[1])),
)


def dft_matrices():
    idx = np.arange(ROWS)
    phase = (idx[:, None] * idx[None, :] % ROWS) * (2.0 * math.pi / ROWS)
    c = np.cos(phase) / math.sqrt(ROWS)
    s = -np.sin(phase) / math.sqrt(ROWS)
    out = []
    for m in (np.block([[c, s], [-s, c]]), np.block([[c, -s], [s, c]])):
        m = m.astype(np.float32)
        hi = m.astype(ml_dtypes.bfloat16)
        lo = (m - hi.astype(np.float32)).astype(ml_dtypes.bfloat16)
        out.append(np.stack([hi, lo]))
    return np.stack(out)


def split(x):
    hi = x.astype(BF16)
    return hi, (x - hi.astype(F32)).astype(BF16)


def split3(x):
    hi = x.astype(BF16)
    rest = x - hi.astype(F32)
    mid = rest.astype(BF16)
    return hi, mid, (rest - mid.astype(F32)).astype(BF16)


def dot(a, b):
    return jnp.dot(a, b, preferred_element_type=F32)


def dot_nt(a, b):
    return lax.dot_general(a, b, (((1,), (1,)), ((), ())), preferred_element_type=F32)


def dot_tn(a, b):
    return lax.dot_general(a, b, (((0,), (0,)), ((), ())), preferred_element_type=F32)


def dot3(a, b):
    return dot(a[0], b[0]) + (dot(a[1], b[0]) + dot(a[0], b[1]))


def device(z, y, x, k):
    return ((y // 2) * 2 + k, z * 8 + (y % 2) * 4 + x)


def kernel(
    pos_s, ang_s, pen_s, obj_h, probe_h, amp_h, prev_h, mult_h, vol_h, mat_h,
    fresh_o, renew_o,
    strip1, strip2, acc1, acc2, zbuf, sharein1, sharein2, stage1, stage2, rsin1, rsin2,
    amp_r, amp_t, probe_v, probe_t, prev_r, mult_r, vol_v, mat_v,
    posb, posr, posall, posm, sums, flips, lbuf, mbuf, nbuf, qbuf, qmat, wfull, vec, qmsg, qflip, qall,
    sem_swap, sem_swap_send, sem_loc, sem_vol, sem_ag_s, sem_ag, sem_sh_s, sem_sh, sem_acc_s, sem_acc,
    sem_rs_s, sem_rs, sem_ln_s, sem_ln, sem_ps_s, sem_ps, sem_q_s, sem_q, sem_smem,
):
    view = lax.axis_index("view")
    tile = lax.axis_index("tile")
    yh, k = view // 2, view % 2
    z, yl, x = tile // 8, (tile // 4) % 2, tile % 4
    y = yh * 2 + yl
    role = z * 8 + k * 4 + x
    own = pl.multiple_of(role * TILE, TILE)
    given = pl.multiple_of(tile * TILE, TILE)
    swapped = yl != k
    partner = device(z, yh * 2 + k, x, yl)
    twin = device(z, y, x, 1 - k)
    fours = range(4)

    def local(src, dst, sem):
        return pltpu.make_async_copy(src, dst, sem)

    def remote(src, dst, send, recv, to):
        return pltpu.make_async_remote_copy(
            src_ref=src, dst_ref=dst, send_sem=send, recv_sem=recv, device_id=to, device_id_type=MESH
        )

    def drain(ref, sem):
        pltpu.make_async_copy(ref, ref, sem).wait()

    def peer(dz, dx):
        return device((z + dz) % 4, y, (x + dx) % 4, k)

    loc = [local(probe_h, probe_v, sem_loc.at[0]), local(mat_h, mat_v, sem_loc.at[1])]
    vols = [
        local(vol_h.at[comp, pl.ds(256 * q, 256)], vol_v.at[comp, pl.ds(256 * q, 256)], sem_vol.at[comp * 4 + q])
        for comp in range(2)
        for q in fours
    ]
    for copy in loc + vols:
        copy.start()

    barrier = pltpu.get_barrier_semaphore()
    greeted = 0
    for dz, dx in PEERS:
        pl.semaphore_signal(barrier, inc=1, device_id=peer(dz, dx), device_id_type=MESH)
        greeted += 1
    for dy in fours:
        for dk in range(2):
            if (dy, dk) != (0, 0):
                pl.semaphore_signal(
                    barrier, inc=1, device_id=device(z, (y + dy) % 4, x, (k + dk) % 2), device_id_type=MESH
                )
                pl.semaphore_signal(
                    barrier, inc=1, device_id=device(3 - z, (y + dy) % 4, 3 - x, (k + dk) % 2), device_id_type=MESH
                )
                greeted += 2
    for p in range(SCANS):
        posb[p : p + 1, :] = jnp.full((1, 128), pos_s[0, p], jnp.int32)
    zeros = jnp.zeros((128, 128), F32)
    for s in range(SCANS):
        for comp in range(2):
            zbuf[s, comp, 0:128] = zeros
            zbuf[s, comp, 256:384] = zeros
    pl.semaphore_wait(barrier, greeted)

    trades = [
        (obj_h, strip1.at[:, pl.ds(given, TILE)], strip1.at[:, pl.ds(own, TILE)]),
        (posb, posr, posr),
        (prev_h, prev_r, prev_r),
        (mult_h, mult_r, mult_r),
        (amp_h, amp_r, amp_r),
    ]

    @pl.when(swapped)
    def _():
        for i, (src, dst, _) in enumerate(trades):
            remote(src, dst, sem_swap_send.at[i], sem_swap.at[i], partner).start()

    @pl.when(jnp.logical_not(swapped))
    def _():
        for i, (src, _, dst) in enumerate(trades):
            local(src, dst, sem_swap.at[i]).start()

    def traded(i):
        drain(trades[i][2], sem_swap.at[i])

    ones8 = jnp.ones((8, 128), BF16)

    def volume_sums(comp):
        col = jnp.zeros((8, 1024), F32)
        for q in fours:
            vols[comp * 4 + q].wait()
            for half in range(2):
                def body(i, carry):
                    col, part = carry
                    base = pl.multiple_of(256 * q + 128 * half + 8 * i, 8)
                    v = vol_v[comp, pl.ds(base, 8), :]
                    r = v[:, 0:128]
                    for j in range(1, 8):
                        r = r + v[:, 128 * j : 128 * j + 128]
                    qmat[pl.ds(pl.multiple_of(8 * i, 8), 8), :] = r
                    return col + v, part

                col, _ = lax.fori_loop(0, 16, body, (col, 0), unroll=4)
                parts = split3(qmat[...])
                line = dot_nt(ones8, parts[0]) + (dot_nt(ones8, parts[1]) + dot_nt(ones8, parts[2]))
                b = 2 * q + half
                sums[2 * comp + 1, b : b + 1, :] = line[0:1]
        for b in range(8):
            sums[2 * comp, b : b + 1, :] = jnp.sum(col[:, 128 * b : 128 * b + 128], axis=0, keepdims=True)

    volume_sums(0)

    def gather_start(strip, n):
        mine = strip.at[:, pl.ds(own, TILE)]
        for j, (dz, dx) in enumerate(PEERS):
            remote(mine, mine, sem_ag_s.at[n], sem_ag.at[n, j], peer(dz, dx)).start()
        remote(mine, mine, sem_sh_s.at[n], sem_sh.at[n], twin).start()

    def gather_finish(strip, n):
        for j in reversed(range(15)):
            dz, dx = PEERS[j]
            src = (z - dz + 4) % 4 * 8 + k * 4 + (x - dx + 4) % 4
            part = strip.at[:, pl.ds(pl.multiple_of(src * TILE, TILE), TILE)]
            drain(part, sem_ag.at[n, j])
            remote(part, part, sem_sh_s.at[n], sem_sh.at[n], twin).start()
        drain(strip.at[0], sem_sh.at[n])

    traded(0)
    gather_start(strip1, 0)

    traded(1)
    to_smem = local(posr, posm, sem_smem)
    to_smem.start()
    local(posr, posall.at[k, z, x], sem_ps.at[6]).start()
    for d in range(1, 4):
        remote(posr, posall.at[k, z, x], sem_ps_s.at[d - 1], sem_ps.at[d - 1], peer(0, d)).start()

    volume_sums(1)

    flat = sums[...].reshape(32, 128)
    rr = lax.broadcasted_iota(jnp.int32, (128, 128), 0)
    cc = lax.broadcasted_iota(jnp.int32, (128, 128), 1)
    anti = jnp.where(rr + cc == 127, 1.0, 0.0).astype(BF16)
    parts = split3(flat)
    turned = dot(parts[0], anti) + (dot(parts[1], anti) + dot(parts[2], anti))
    for a in fours:
        for b in range(8):
            flips[a, 7 - b : 8 - b, :] = turned[8 * a + b : 8 * a + b + 1]
    lane = lax.broadcasted_iota(jnp.int32, (8, 128), 1)
    scale = 1.0 / math.sqrt(TOTAL)
    whole = [jnp.sum(jnp.sum(sums[2 * c], axis=1, keepdims=True), axis=0, keepdims=True) * scale for c in range(2)]
    for u in fours:
        angle = ang_s[u]
        lines = []
        for c in range(2):
            lines.append(
                jnp.where(
                    angle == 0,
                    sums[2 * c],
                    jnp.where(angle == 1, sums[2 * c + 1], jnp.where(angle == 2, flips[2 * c], flips[2 * c + 1])),
                )
                * scale
            )
        for j in fours:
            re = lines[0] if j == 0 else pltpu.roll(lines[0], 128 - 32 * j, 1)
            im = lines[1] if j == 1 else pltpu.roll(lines[1], (160 - 32 * j) % 128, 1)
            rows = jnp.where(
                lane < 32,
                re,
                jnp.where(lane < 64, im, jnp.where(lane == 64, whole[0], whole[1])),
            )
            for b in range(8):
                e = (u // 2 * 2 + b % 2) * 2 + u % 2
                lbuf[j, b // 2, e] = rows[b : b + 1]
    local(lbuf.at[x], mbuf.at[x], sem_ln.at[0, 3]).start()
    for d in range(1, 4):
        xd = (x + d) % 4
        remote(lbuf.at[xd], mbuf.at[x], sem_ln_s.at[0, d - 1], sem_ln.at[0, d - 1], peer(0, d)).start()

    for copy in loc:
        copy.wait()
    for comp in range(2):
        probe_t[comp] = probe_v[comp].T
    to_smem.wait()

    gather_finish(strip1, 0)

    for d in range(1, 4):
        drain(posr, sem_ps.at[d - 1])
    drain(posr, sem_ps.at[6])
    for d in range(1, 4):
        remote(posall.at[k, z], posall.at[k, z], sem_ps_s.at[2 + d], sem_ps.at[2 + d], peer(d, 0)).start()

    pr, pi = probe_t[0], probe_t[1]

    traded(4)
    for s in range(SCANS):
        amp_t[s // 2, :, (s % 2) * 128 : (s % 2) * 128 + 128] = amp_r[s].T

    def compute(strip):
        forward = (mat_v[0, 0], mat_v[0, 1])
        inverse = (mat_v[1, 0], mat_v[1, 1])
        pr, pi = probe_t[0], probe_t[1]

        def pair(p, carry):
            exits = []
            for i in range(2):
                start = posm[2 * p + i, 0]
                wr = strip[0, pl.ds(start, 128), :]
                wi = strip[1, pl.ds(start, 128), :]
                exits.append(jnp.concatenate([pr * wr - pi * wi, pr * wi + pi * wr], axis=1))
            a = dot3(split(jnp.concatenate(exits, axis=0)), forward)
            a = jnp.concatenate(
                [
                    jnp.concatenate([a[:128, :128], a[128:, :128]], axis=1),
                    jnp.concatenate([a[:128, 128:], a[128:, 128:]], axis=1),
                ],
                axis=0,
            )
            f = dot3(inverse, split(a))
            fr, fi = f[:128], f[128:]
            g = amp_t[p] * lax.rsqrt(jnp.maximum(fr * fr + fi * fi, FLOOR * FLOOR))
            h = dot3(forward, split(jnp.concatenate([fr * g, fi * g], axis=0)))
            h = jnp.concatenate(
                [
                    jnp.concatenate([h[:128, :128], h[128:, :128]], axis=1),
                    jnp.concatenate([h[:128, 128:], h[128:, 128:]], axis=1),
                ],
                axis=0,
            )
            b = dot3(split(h), inverse)
            for i in range(2):
                br, bi = b[128 * i : 128 * i + 128, :128], b[128 * i : 128 * i + 128, 128:]
                zbuf[2 * p + i, 0, 128:256] = pr * br + pi * bi
                zbuf[2 * p + i, 1, 128:256] = pr * bi - pi * br
            return carry

        lax.fori_loop(0, SCANS // 2, pair, 0)

    def own_weight():
        return wfull[role // 4, pl.ds(pl.multiple_of(role % 4 * 32, 32), 32), :]

    def block_sum(comp, b):
        total = None
        for s in range(SCANS):
            off = jnp.clip(128 + 128 * b - posm[s, 0], 0, 256)
            part = zbuf[s, comp, pl.ds(off, 128), :]
            total = part if total is None else total + part
        return total

    def scatter_start(acc, sharein, stage, n, rho, messages):
        height = stage.shape[2]
        if messages:
            vec[...] = jnp.zeros((8, 128), F32)
            for comp in range(2):
                extra = mult_r[comp] / rho + (rho * prev_r[comp] - mult_r[comp]) * own_weight()
                vec[comp : comp + 1, :] = jnp.sum(extra, axis=0, keepdims=True)
        for which in (1 - k, k):
            def body(j, carry, which=which):
                b = 2 * j + which
                for comp in range(2):
                    total = block_sum(comp, b)
                    acc[which, j, comp] = total
                    if messages:
                        vec[comp : comp + 1, :] += jnp.sum(total * wfull[b], axis=0, keepdims=True)
                return carry
            for j in fours:
                body(j, 0)
                if which is not k:
                    remote(acc.at[which, j], sharein.at[j], sem_acc_s.at[n], sem_acc.at[n, j], twin).start()
        for i in fours:
            zd = (z + (2, 1, 3, 0)[i]) % 4
            drain(sharein.at[zd], sem_acc.at[n, zd])
            for xd in fours:
                for comp in range(2):
                    rows = slice(32 * xd, 32 * xd + 32)
                    stage[zd, xd, 32 * comp : 32 * comp + 32] = acc[k, zd, comp, rows] + sharein[zd, comp, rows]
                if messages:
                    stage[zd, xd, 64:72] = vec[...]
            dz = (2, 1, 3, 0)[i]
            if dz == 0:
                for comp in range(2):
                    rows = slice(32 * comp, 32 * comp + 32)
                    stage[z, x, rows] = stage[z, x, rows] + (rho * prev_r[comp] - mult_r[comp])
            for dx in (2, 1, 3, 0):
                if (dz, dx) != (0, 0):
                    j = PEERS.index((dz, dx))
                    remote(
                        stage.at[zd, (x + dx) % 4], scatter_in[n].at[j], sem_rs_s.at[n], sem_rs.at[n], peer(dz, dx),
                    ).start()

    scatter_in = (rsin1, rsin2)

    def scatter_finish(stage, n):
        drain(scatter_in[n].at[pl.ds(0, 15)], sem_rs.at[n])
        total = stage[z, x]
        for j in range(15):
            total = total + scatter_in[n][j]
        return total

    rho = jnp.full((32, 128), pen_s[0], jnp.int32).astype(F32) / jnp.full((32, 128), pen_s[1], jnp.int32).astype(F32)

    compute(strip1)
    traded(2)
    traded(3)
    scatter_start(acc1, sharein1, stage1, 0, rho, False)

    for d in range(1, 4):
        drain(posall.at[k, z], sem_ps.at[2 + d])
    remote(posall.at[k], posall.at[k], sem_ps_s.at[6], sem_ps.at[7], twin).start()
    for d in range(4):
        drain(mbuf.at[0], sem_ln.at[0, d])
    local(mbuf.at[:, z], nbuf.at[z], sem_ln.at[1, 3]).start()
    for d in range(1, 4):
        zd = (z + d) % 4
        remote(mbuf.at[:, zd], nbuf.at[z], sem_ln_s.at[1, d - 1], sem_ln.at[1, d - 1], peer(d, 0)).start()

    drain(posall.at[0], sem_ps.at[7])
    where = posall[...].reshape(256, 128)
    lanes = lax.broadcasted_iota(jnp.int32, (256, 128), 1)
    high = jnp.where(lanes == (where >> 7), 1.0, 0.0)
    low = jnp.where(lanes == ((128 - (where & 127)) & 127), 1.0, 0.0)
    counts = dot_tn(high.astype(BF16), low.astype(BF16))
    power = split(pr * pr + pi * pi)
    before = jnp.zeros((128, 128), F32)
    for b in range(8):
        here = pltpu.roll(jnp.broadcast_to(counts[b : b + 1], (128, 128)), 0, 1, stride=1, stride_axis=0)
        toeplitz = jnp.where(rr >= cc, here, before).astype(BF16)
        before = here
        wfull[b] = 1.0 / (dot(toeplitz, power[0]) + dot(toeplitz, power[1]) + rho[0:1])
    weight = own_weight()

    total = scatter_finish(stage1, 0)
    for comp in range(2):
        strip2[comp, pl.ds(own, TILE), :] = total[32 * comp : 32 * comp + 32] * weight
    gather_start(strip2, 1)
    for d in range(4):
        drain(nbuf.at[0], sem_ln.at[1, d])
    e = y * 2 + k
    local(nbuf.at[:, :, e], qbuf.at[yh * 2 + k, :, yl], sem_ln.at[2, 7]).start()
    i = 0
    for dy in fours:
        for dk in range(2):
            if (dy, dk) != (0, 0):
                yd, kd = (y + dy) % 4, (k + dk) % 2
                remote(
                    nbuf.at[:, :, yd * 2 + kd], qbuf.at[yh * 2 + k, :, yl],
                    sem_ln_s.at[2, i], sem_ln.at[2, i], device(z, yd, x, kd),
                ).start()
                i += 1
    gather_finish(strip2, 1)

    compute(strip2)
    scatter_start(acc2, sharein2, stage2, 1, rho, True)

    for d in range(8):
        drain(nbuf.at[:, :, 0], sem_ln.at[2, d])
    for h in range(128):
        qmat[h : h + 1, :] = qbuf[h // 32, h // 8 % 4, h // 4 % 2, h % 4]
    lines = qmat[...].T

    total = scatter_finish(stage2, 1)
    for comp in range(2):
        rows = slice(32 * comp, 32 * comp + 32)
        qmsg[rows] = total[rows] * weight + mult_r[comp] / rho
    qmsg[64:72] = total[64:72]
    for comp in range(2):
        for i in range(32):
            qflip[32 * comp + 31 - i : 32 * comp + 32 - i] = qmsg[32 * comp + i : 32 * comp + i + 1]
    qflip[64:72] = total[64:72]
    for u in fours:
        to = device(3 - z, u // 2 * 2 + 1 - k, 3 - x, u % 2)
        remote(qflip, qall.at[4 + y], sem_q_s.at[0], sem_q, to).start()
    for i in range(3):
        d = i + 1
        yd, kd = ((yh + d // 2) % 2) * 2 + k, (k + d % 2) % 2
        remote(qmsg, qall.at[y], sem_q_s.at[1], sem_q, device(z, yd, x, kd)).start()

    @pl.when(swapped)
    def _():
        remote(qmsg, qall.at[y], sem_q_s.at[2], sem_q, device(z, yh * 2 + k, x, k)).start()

    @pl.when(jnp.logical_not(swapped))
    def _():
        local(qmsg, qall.at[y], sem_q).start()

    drain(qall, sem_q)
    qs, qm = qall.at[pl.ds(0, 4)], qall.at[pl.ds(4, 4)]

    mine = ang_s[yh * 2 + k]
    same = [jnp.where(ang_s[u] == mine, 1.0, 0.0) for u in fours]
    turned = [jnp.where(ang_s[u] == lax.rem(mine + 2, 4), 1.0, 0.0) for u in fours]
    other = [1.0 - same[u] - turned[u] for u in fours]
    members = same[0] + same[1] + same[2] + same[3] + turned[0] + turned[1] + turned[2] + turned[3]
    for comp in range(2):
        rows = slice(32 * comp, 32 * comp + 32)
        line = lines[rows]
        spread = (4.0 - members) * lines[64 + comp : 65 + comp]
        mix = members * line
        for u in fours:
            mix = mix - same[u] * qs[u, rows] - turned[u] * qm[u, rows]
            spread = spread - other[u] * (qs[u, 64 + comp : 65 + comp] + qm[u, 64 + comp : 65 + comp])
        fresh = line - 0.25 * (mix + spread * (1.0 / TOTAL))
        fresh_o[comp] = fresh
        keep = jnp.zeros((32, 128), F32)
        for u in fours:
            keep = keep + jnp.where(yh * 2 + k == u, qs[u, rows], 0.0)
        renew_o[comp] = rho * (keep - fresh)

    @pl.when(swapped)
    def _():
        for i, (src, _, dst) in enumerate(trades):
            drain(dst, sem_swap_send.at[i])
        drain(qmsg, sem_q_s.at[2])

    drain(qs, sem_q_s.at[0])
    drain(qs.at[pl.ds(0, 3)], sem_q_s.at[1])
    for n, strip in ((0, strip1), (1, strip2)):
        drain(strip.at[0, pl.ds(0, 960)], sem_ag_s.at[n])
        drain(strip.at[0], sem_sh_s.at[n])
        drain(scatter_in[n].at[pl.ds(0, 15)], sem_rs_s.at[n])
        drain((sharein1, sharein2)[n], sem_acc_s.at[n])
    for d in range(3):
        drain(posr, sem_ps_s.at[d])
        drain(posall.at[k, z], sem_ps_s.at[3 + d])
        drain(lbuf.at[0], sem_ln_s.at[0, d])
        drain(nbuf.at[0], sem_ln_s.at[1, d])
    drain(posall.at[0], sem_ps_s.at[6])
    for d in range(7):
        drain(nbuf.at[:, :, 0], sem_ln_s.at[2, d])


def shards(objects, probe, positions, amplitudes, reproj_prev, multipliers, volume, angles, penalty):
    across = lambda a: jnp.transpose(a[0], (0, 2, 1))
    any_, vmem, smem = (pl.BlockSpec(memory_space=m) for m in (pl.ANY, pltpu.VMEM, pltpu.SMEM))
    mats = jnp.asarray(dft_matrices())
    dma = pltpu.SemaphoreType.DMA
    out = jax.ShapeDtypeStruct((2, TILE, ROWS), F32)
    scratch = [
        pltpu.VMEM((2, TOTAL, ROWS), F32),
        pltpu.VMEM((2, TOTAL, ROWS), F32),
        pltpu.VMEM((2, 4, 2, 128, 128), F32),
        pltpu.VMEM((2, 4, 2, 128, 128), F32),
        pltpu.VMEM((SCANS, 2, 384, 128), F32),
        pltpu.VMEM((4, 2, 128, 128), F32),
        pltpu.VMEM((4, 2, 128, 128), F32),
        pltpu.VMEM((4, 4, 64, 128), F32),
        pltpu.VMEM((4, 4, 72, 128), F32),
        pltpu.VMEM((16, 64, 128), F32),
        pltpu.VMEM((16, 72, 128), F32),
        pltpu.VMEM((SCANS, 128, 128), F32),
        pltpu.VMEM((SCANS // 2, 128, 256), F32),
        pltpu.VMEM((2, 128, 128), F32),
        pltpu.VMEM((2, 128, 128), F32),
        pltpu.VMEM((2, TILE, ROWS), F32),
        pltpu.VMEM((2, TILE, ROWS), F32),
        pltpu.VMEM((2, TOTAL, TOTAL), F32),
        pltpu.VMEM((2, 2, 256, 256), BF16),
        pltpu.VMEM((SCANS, 128), jnp.int32),
        pltpu.VMEM((SCANS, 128), jnp.int32),
        pltpu.VMEM((2, 4, 4, SCANS, 128), jnp.int32),
        pltpu.SMEM((SCANS, 128), jnp.int32),
        pltpu.VMEM((4, 8, 128), F32),
        pltpu.VMEM((4, 8, 128), F32),
        pltpu.VMEM((4, 4, 8, 1, 128), F32),
        pltpu.VMEM((4, 4, 8, 1, 128), F32),
        pltpu.VMEM((4, 4, 8, 1, 128), F32),
        pltpu.VMEM((4, 4, 2, 4, 1, 128), F32),
        pltpu.VMEM((128, 128), F32),
        pltpu.VMEM((8, 128, 128), F32),
        pltpu.VMEM((8, 128), F32),
        pltpu.VMEM((72, 128), F32),
        pltpu.VMEM((72, 128), F32),
        pltpu.VMEM((8, 72, 128), F32),
        dma((5,)), dma((5,)), dma((2,)), dma((8,)),
        dma((2,)), dma((2, 15)), dma((2,)), dma((2,)),
        dma((2,)), dma((2, 4)), dma((2,)), dma((2,)),
        dma((3, 8)), dma((3, 8)), dma((8,)), dma((8,)),
        dma((3,)), dma, dma,
    ]
    fresh, renewed = pl.pallas_call(
        kernel,
        out_shape=(out, out),
        in_specs=[smem, smem, smem] + [any_] * 7,
        out_specs=(vmem, vmem),
        scratch_shapes=scratch,
        compiler_params=pltpu.CompilerParams(
            collective_id=0, has_side_effects=True, vmem_limit_bytes=60 * 1024 * 1024
        ),
    )(
        positions,
        angles,
        penalty,
        across(objects),
        probe,
        amplitudes[0],
        across(reproj_prev),
        across(multipliers),
        volume[:, 0],
        mats,
    )
    back = lambda a: jnp.transpose(a, (0, 2, 1))[None]
    return back(fresh), back(renewed)


def solution(mesh):
    return jax.shard_map(
        shards,
        mesh=mesh,
        in_specs=(
            P("view", None, None, "tile"),
            P(),
            P("view", "tile"),
            P("view", "tile", None, None),
            P("view", None, None, "tile"),
            P("view", None, None, "tile"),
            P(None, ("view", "tile"), None, None),
            P(),
            P(),
        ),
        out_specs=(P("view", None, None, "tile"), P("view", None, None, "tile")),
        check_vma=False,
    )
```

```python
import math

import jax
import jax.numpy as jnp
import ml_dtypes
import numpy as np
from jax import lax
from jax.experimental import pallas as pl
from jax.experimental.pallas import tpu as pltpu
from jax.sharding import PartitionSpec as P

ITERS = 2
F32 = jnp.float32
BF16 = jnp.bfloat16
MESH = pl.DeviceIdType.MESH

ROWS = 128
TOTAL = 1024
SCANS = 8
TILE = 32
FLOOR = 0.25 / math.sqrt(SCANS * 32 * ROWS // TOTAL)

PEERS = sorted(
    [(dz, dx) for dz in range(4) for dx in range(4) if (dz, dx) != (0, 0)],
    key=lambda p: -(min(p[0], 4 - p[0]) + min(p[1], 4 - p[1])),
)


def dft_matrices():
    idx = np.arange(ROWS)
    phase = (idx[:, None] * idx[None, :] % ROWS) * (2.0 * math.pi / ROWS)
    c = np.cos(phase) / math.sqrt(ROWS)
    s = -np.sin(phase) / math.sqrt(ROWS)
    out = []
    for m in (np.block([[c, s], [-s, c]]), np.block([[c, -s], [s, c]])):
        m = m.astype(np.float32)
        hi = m.astype(ml_dtypes.bfloat16)
        lo = (m - hi.astype(np.float32)).astype(ml_dtypes.bfloat16)
        out.append(np.stack([hi, lo]))
    return np.stack(out)


def split(x):
    hi = x.astype(BF16)
    return hi, (x - hi.astype(F32)).astype(BF16)


def split3(x):
    hi = x.astype(BF16)
    rest = x - hi.astype(F32)
    mid = rest.astype(BF16)
    return hi, mid, (rest - mid.astype(F32)).astype(BF16)


def dot(a, b):
    return jnp.dot(a, b, preferred_element_type=F32)


def dot_nt(a, b):
    return lax.dot_general(a, b, (((1,), (1,)), ((), ())), preferred_element_type=F32)


def dot_tn(a, b):
    return lax.dot_general(a, b, (((0,), (0,)), ((), ())), preferred_element_type=F32)


def dot3(a, b):
    return dot(a[0], b[0]) + (dot(a[1], b[0]) + dot(a[0], b[1]))


def device(z, y, x, k):
    return ((y // 2) * 2 + k, z * 8 + (y % 2) * 4 + x)


def kernel(
    pos_s, ang_s, pen_s, obj_h, probe_h, amp_h, prev_h, mult_h, vol_h, mat_h,
    fresh_o, renew_o,
    strip1, strip2, acc1, acc2, zbuf, sharein1, sharein2, stage1, stage2, rsin1, rsin2,
    amp_r, amp_t, probe_v, probe_t, prev_r, mult_r, vol_v, mat_v,
    posb, posr, posall, posm, sums, flips, lbuf, mbuf, nbuf, qbuf, qmat, wfull, vec, qmsg, qflip, qall,
    sem_swap, sem_swap_send, sem_loc, sem_vol, sem_ag_s, sem_ag, sem_sh_s, sem_sh, sem_acc_s, sem_acc,
    sem_rs_s, sem_rs, sem_ln_s, sem_ln, sem_ps_s, sem_ps, sem_q_s, sem_q, sem_smem,
):
    view = lax.axis_index("view")
    tile = lax.axis_index("tile")
    yh, k = view // 2, view % 2
    z, yl, x = tile // 8, (tile // 4) % 2, tile % 4
    y = yh * 2 + yl
    role = z * 8 + k * 4 + x
    own = pl.multiple_of(role * TILE, TILE)
    given = pl.multiple_of(tile * TILE, TILE)
    swapped = yl != k
    partner = device(z, yh * 2 + k, x, yl)
    twin = device(z, y, x, 1 - k)
    fours = range(4)

    def local(src, dst, sem):
        return pltpu.make_async_copy(src, dst, sem)

    def remote(src, dst, send, recv, to):
        return pltpu.make_async_remote_copy(
            src_ref=src, dst_ref=dst, send_sem=send, recv_sem=recv, device_id=to, device_id_type=MESH
        )

    def drain(ref, sem):
        pltpu.make_async_copy(ref, ref, sem).wait()

    def peer(dz, dx):
        return device((z + dz) % 4, y, (x + dx) % 4, k)

    loc = [local(probe_h, probe_v, sem_loc.at[0]), local(mat_h, mat_v, sem_loc.at[1])]
    vols = [
        local(vol_h.at[comp, pl.ds(256 * q, 256)], vol_v.at[comp, pl.ds(256 * q, 256)], sem_vol.at[comp * 4 + q])
        for comp in range(2)
        for q in fours
    ]
    for copy in loc + vols:
        copy.start()

    barrier = pltpu.get_barrier_semaphore()
    greeted = 0
    for dz, dx in PEERS:
        pl.semaphore_signal(barrier, inc=1, device_id=peer(dz, dx), device_id_type=MESH)
        greeted += 1
    for dy in fours:
        for dk in range(2):
            if (dy, dk) != (0, 0):
                pl.semaphore_signal(
                    barrier, inc=1, device_id=device(z, (y + dy) % 4, x, (k + dk) % 2), device_id_type=MESH
                )
                pl.semaphore_signal(
                    barrier, inc=1, device_id=device(3 - z, (y + dy) % 4, 3 - x, (k + dk) % 2), device_id_type=MESH
                )
                greeted += 2
    for p in range(SCANS):
        posb[p : p + 1, :] = jnp.full((1, 128), pos_s[0, p], jnp.int32)
    zeros = jnp.zeros((128, 128), F32)
    for s in range(SCANS):
        for comp in range(2):
            zbuf[s, comp, 0:128] = zeros
            zbuf[s, comp, 256:384] = zeros
    pl.semaphore_wait(barrier, greeted)

    trades = [
        (obj_h, strip1.at[:, pl.ds(given, TILE)], strip1.at[:, pl.ds(own, TILE)]),
        (posb, posr, posr),
        (prev_h, prev_r, prev_r),
        (mult_h, mult_r, mult_r),
        (amp_h, amp_r, amp_r),
    ]

    def start_trade(i):
        src, there, here = trades[i]

        @pl.when(swapped)
        def _():
            remote(src, there, sem_swap_send.at[i], sem_swap.at[i], partner).start()

        @pl.when(jnp.logical_not(swapped))
        def _():
            local(src, here, sem_swap.at[i]).start()

    for i in range(4):
        start_trade(i)

    def traded(i):
        drain(trades[i][2], sem_swap.at[i])

    ones8 = jnp.ones((8, 128), BF16)

    def volume_sums(comp):
        col = jnp.zeros((8, 1024), F32)
        for q in fours:
            vols[comp * 4 + q].wait()
            for half in range(2):
                def body(i, carry):
                    col, part = carry
                    base = pl.multiple_of(256 * q + 128 * half + 8 * i, 8)
                    v = vol_v[comp, pl.ds(base, 8), :]
                    r = v[:, 0:128]
                    for j in range(1, 8):
                        r = r + v[:, 128 * j : 128 * j + 128]
                    qmat[pl.ds(pl.multiple_of(8 * i, 8), 8), :] = r
                    return col + v, part

                col, _ = lax.fori_loop(0, 16, body, (col, 0), unroll=4)
                parts = split3(qmat[...])
                line = dot_nt(ones8, parts[0]) + (dot_nt(ones8, parts[1]) + dot_nt(ones8, parts[2]))
                b = 2 * q + half
                sums[2 * comp + 1, b : b + 1, :] = line[0:1]
        for b in range(8):
            sums[2 * comp, b : b + 1, :] = jnp.sum(col[:, 128 * b : 128 * b + 128], axis=0, keepdims=True)

    volume_sums(0)

    def gather_start(strip, n, comp):
        mine = strip.at[comp, pl.ds(own, TILE)]
        for j, (dz, dx) in enumerate(PEERS):
            remote(mine, mine, sem_ag_s.at[n], sem_ag.at[n, comp, j], peer(dz, dx)).start()
        remote(mine, mine, sem_sh_s.at[n], sem_sh.at[n], twin).start()

    def gather_finish(strip, n):
        for comp in range(2):
            for j in reversed(range(15)):
                dz, dx = PEERS[j]
                src = (z - dz + 4) % 4 * 8 + k * 4 + (x - dx + 4) % 4
                part = strip.at[comp, pl.ds(pl.multiple_of(src * TILE, TILE), TILE)]
                drain(part, sem_ag.at[n, comp, j])
                remote(part, part, sem_sh_s.at[n], sem_sh.at[n], twin).start()
        drain(strip.at[0], sem_sh.at[n])

    traded(0)
    for comp in range(2):
        gather_start(strip1, 0, comp)
    start_trade(4)

    traded(1)
    to_smem = local(posr, posm, sem_smem)
    to_smem.start()
    local(posr, posall.at[k, z, x], sem_ps.at[6]).start()
    for d in range(1, 4):
        remote(posr, posall.at[k, z, x], sem_ps_s.at[d - 1], sem_ps.at[d - 1], peer(0, d)).start()

    volume_sums(1)

    flat = sums[...].reshape(32, 128)
    rr = lax.broadcasted_iota(jnp.int32, (128, 128), 0)
    cc = lax.broadcasted_iota(jnp.int32, (128, 128), 1)
    anti = jnp.where(rr + cc == 127, 1.0, 0.0).astype(BF16)
    parts = split3(flat)
    turned = dot(parts[0], anti) + (dot(parts[1], anti) + dot(parts[2], anti))
    for a in fours:
        for b in range(8):
            flips[a, 7 - b : 8 - b, :] = turned[8 * a + b : 8 * a + b + 1]
    lane = lax.broadcasted_iota(jnp.int32, (8, 128), 1)
    scale = 1.0 / math.sqrt(TOTAL)
    whole = [jnp.sum(jnp.sum(sums[2 * c], axis=1, keepdims=True), axis=0, keepdims=True) * scale for c in range(2)]
    for u in fours:
        angle = ang_s[u]
        lines = []
        for c in range(2):
            lines.append(
                jnp.where(
                    angle == 0,
                    sums[2 * c],
                    jnp.where(angle == 1, sums[2 * c + 1], jnp.where(angle == 2, flips[2 * c], flips[2 * c + 1])),
                )
                * scale
            )
        for j in fours:
            re = lines[0] if j == 0 else pltpu.roll(lines[0], 128 - 32 * j, 1)
            im = lines[1] if j == 1 else pltpu.roll(lines[1], (160 - 32 * j) % 128, 1)
            rows = jnp.where(
                lane < 32,
                re,
                jnp.where(lane < 64, im, jnp.where(lane == 64, whole[0], whole[1])),
            )
            for b in range(8):
                e = (u // 2 * 2 + b % 2) * 2 + u % 2
                lbuf[j, b // 2, e] = rows[b : b + 1]
    local(lbuf.at[x], mbuf.at[x], sem_ln.at[0, 3]).start()
    for d in range(1, 4):
        xd = (x + d) % 4
        remote(lbuf.at[xd], mbuf.at[x], sem_ln_s.at[0, d - 1], sem_ln.at[0, d - 1], peer(0, d)).start()

    for copy in loc:
        copy.wait()
    for comp in range(2):
        probe_t[comp] = probe_v[comp].T
    to_smem.wait()

    gather_finish(strip1, 0)

    for d in range(1, 4):
        drain(posr, sem_ps.at[d - 1])
    drain(posr, sem_ps.at[6])
    for d in range(1, 4):
        remote(posall.at[k, z], posall.at[k, z], sem_ps_s.at[2 + d], sem_ps.at[2 + d], peer(d, 0)).start()

    pr, pi = probe_t[0], probe_t[1]

    traded(4)
    for s in range(SCANS):
        amp_t[s // 2, :, (s % 2) * 128 : (s % 2) * 128 + 128] = amp_r[s].T

    def compute(strip):
        forward = (mat_v[0, 0], mat_v[0, 1])
        inverse = (mat_v[1, 0], mat_v[1, 1])
        pr, pi = probe_t[0], probe_t[1]

        def pair(p, carry):
            exits = []
            for i in range(2):
                start = posm[2 * p + i, 0]
                wr = strip[0, pl.ds(start, 128), :]
                wi = strip[1, pl.ds(start, 128), :]
                exits.append(jnp.concatenate([pr * wr - pi * wi, pr * wi + pi * wr], axis=1))
            a = dot3(split(jnp.concatenate(exits, axis=0)), forward)
            a = jnp.concatenate(
                [
                    jnp.concatenate([a[:128, :128], a[128:, :128]], axis=1),
                    jnp.concatenate([a[:128, 128:], a[128:, 128:]], axis=1),
                ],
                axis=0,
            )
            f = dot3(inverse, split(a))
            fr, fi = f[:128], f[128:]
            g = amp_t[p] * lax.rsqrt(jnp.maximum(fr * fr + fi * fi, FLOOR * FLOOR))
            h = dot3(forward, split(jnp.concatenate([fr * g, fi * g], axis=0)))
            h = jnp.concatenate(
                [
                    jnp.concatenate([h[:128, :128], h[128:, :128]], axis=1),
                    jnp.concatenate([h[:128, 128:], h[128:, 128:]], axis=1),
                ],
                axis=0,
            )
            b = dot3(split(h), inverse)
            for i in range(2):
                br, bi = b[128 * i : 128 * i + 128, :128], b[128 * i : 128 * i + 128, 128:]
                zbuf[2 * p + i, 0, 128:256] = pr * br + pi * bi
                zbuf[2 * p + i, 1, 128:256] = pr * bi - pi * br
            return carry

        lax.fori_loop(0, SCANS // 2, pair, 0, unroll=True)

    def own_weight():
        return wfull[role // 4, pl.ds(pl.multiple_of(role % 4 * 32, 32), 32), :]

    def block_sum(comp, b):
        total = None
        for s in range(SCANS):
            off = jnp.clip(128 + 128 * b - posm[s, 0], 0, 256)
            part = zbuf[s, comp, pl.ds(off, 128), :]
            total = part if total is None else total + part
        return total

    def scatter_start(acc, sharein, stage, n, rho):
        if n:
            vec[...] = jnp.zeros((8, 128), F32)
            for comp in range(2):
                extra = mult_r[comp] / rho + (rho * prev_r[comp] - mult_r[comp]) * own_weight()
                vec[comp : comp + 1, :] = jnp.sum(extra, axis=0, keepdims=True)

        def blocks(comp, parity):
            for j in fours:
                i = 2 * j + parity
                total = block_sum(comp, i)
                acc[parity, comp, j] = total
                if n:
                    vec[comp : comp + 1, :] += jnp.sum(total * wfull[i], axis=0, keepdims=True)

        for comp in range(2):
            blocks(comp, 1 - k)
            remote(acc.at[1 - k, comp], sharein.at[comp], sem_acc_s.at[n], sem_acc.at[n, comp], twin).start()
        for comp in range(2):
            blocks(comp, k)
            drain(sharein.at[comp], sem_acc.at[n, comp])
            for zd in fours:
                for xd in fours:
                    rows = slice(32 * xd, 32 * xd + 32)
                    stage[comp, zd, xd, 0:32] = acc[k, comp, zd, rows] + sharein[comp, zd, rows]
                    if n and comp:
                        stage[comp, zd, xd, 32:40] = vec[...]
            mine = pl.ds(0, 32)
            stage[comp, z, x, mine] = stage[comp, z, x, mine] + (rho * prev_r[comp] - mult_r[comp])
            height = 40 if n and comp else 32
            for j, (dz, dx) in enumerate(PEERS):
                remote(
                    stage.at[comp, (z + dz) % 4, (x + dx) % 4, pl.ds(0, height)],
                    scatter_in[n].at[comp, j, pl.ds(0, height)],
                    sem_rs_s.at[n, comp], sem_rs.at[n, comp], peer(dz, dx),
                ).start()

    scatter_in = (rsin1, rsin2)

    def arrived(n, comp):
        return scatter_in[n].at[comp, :, pl.ds(0, 40 if n and comp else 32)]

    def scatter_finish(stage, n, comp):
        drain(arrived(n, comp), sem_rs.at[n, comp])
        height = 40 if n and comp else 32
        total = stage[comp, z, x, 0:height]
        for j in range(15):
            total = total + scatter_in[n][comp, j, 0:height]
        return total

    rho = jnp.full((32, 128), pen_s[0], jnp.int32).astype(F32) / jnp.full((32, 128), pen_s[1], jnp.int32).astype(F32)

    compute(strip1)
    traded(2)
    traded(3)
    scatter_start(acc1, sharein1, stage1, 0, rho)

    for d in range(1, 4):
        drain(posall.at[k, z], sem_ps.at[2 + d])
    remote(posall.at[k], posall.at[k], sem_ps_s.at[6], sem_ps.at[7], twin).start()
    for d in range(4):
        drain(mbuf.at[0], sem_ln.at[0, d])
    local(mbuf.at[:, z], nbuf.at[z], sem_ln.at[1, 3]).start()
    for d in range(1, 4):
        zd = (z + d) % 4
        remote(mbuf.at[:, zd], nbuf.at[z], sem_ln_s.at[1, d - 1], sem_ln.at[1, d - 1], peer(d, 0)).start()

    drain(posall.at[0], sem_ps.at[7])
    where = posall[...].reshape(256, 128)
    lanes = lax.broadcasted_iota(jnp.int32, (256, 128), 1)
    high = jnp.where(lanes == (where >> 7), 1.0, 0.0)
    low = jnp.where(lanes == ((128 - (where & 127)) & 127), 1.0, 0.0)
    counts = dot_tn(high.astype(BF16), low.astype(BF16))
    power = split(pr * pr + pi * pi)
    before = jnp.zeros((128, 128), F32)
    for b in range(8):
        here = pltpu.roll(jnp.broadcast_to(counts[b : b + 1], (128, 128)), 0, 1, stride=1, stride_axis=0)
        toeplitz = jnp.where(rr >= cc, here, before).astype(BF16)
        before = here
        wfull[b] = 1.0 / (dot(toeplitz, power[0]) + dot(toeplitz, power[1]) + rho[0:1])
    weight = own_weight()

    for comp in range(2):
        strip2[comp, pl.ds(own, TILE), :] = scatter_finish(stage1, 0, comp) * weight
        gather_start(strip2, 1, comp)
    for d in range(4):
        drain(nbuf.at[0], sem_ln.at[1, d])
    e = y * 2 + k
    local(nbuf.at[:, :, e], qbuf.at[yh * 2 + k, :, yl], sem_ln.at[2, 7]).start()
    i = 0
    for dy in fours:
        for dk in range(2):
            if (dy, dk) != (0, 0):
                yd, kd = (y + dy) % 4, (k + dk) % 2
                remote(
                    nbuf.at[:, :, yd * 2 + kd], qbuf.at[yh * 2 + k, :, yl],
                    sem_ln_s.at[2, i], sem_ln.at[2, i], device(z, yd, x, kd),
                ).start()
                i += 1
    gather_finish(strip2, 1)

    compute(strip2)
    scatter_start(acc2, sharein2, stage2, 1, rho)

    for d in range(8):
        drain(nbuf.at[:, :, 0], sem_ln.at[2, d])
    for h in range(128):
        qmat[h : h + 1, :] = qbuf[h // 32, h // 8 % 4, h // 4 % 2, h % 4]
    lines = qmat[...].T

    for comp in range(2):
        total = scatter_finish(stage2, 1, comp)
        qmsg[32 * comp : 32 * comp + 32] = total[0:32] * weight + mult_r[comp] / rho
    qmsg[64:72] = total[32:40]
    for comp in range(2):
        for i in range(32):
            qflip[32 * comp + 31 - i : 32 * comp + 32 - i] = qmsg[32 * comp + i : 32 * comp + i + 1]
    qflip[64:72] = total[32:40]
    for u in fours:
        to = device(3 - z, u // 2 * 2 + 1 - k, 3 - x, u % 2)
        remote(qflip, qall.at[4 + y], sem_q_s.at[0], sem_q, to).start()
    for i in range(3):
        d = i + 1
        yd, kd = ((yh + d // 2) % 2) * 2 + k, (k + d % 2) % 2
        remote(qmsg, qall.at[y], sem_q_s.at[1], sem_q, device(z, yd, x, kd)).start()

    @pl.when(swapped)
    def _():
        remote(qmsg, qall.at[y], sem_q_s.at[2], sem_q, device(z, yh * 2 + k, x, k)).start()

    @pl.when(jnp.logical_not(swapped))
    def _():
        local(qmsg, qall.at[y], sem_q).start()

    drain(qall, sem_q)
    qs, qm = qall.at[pl.ds(0, 4)], qall.at[pl.ds(4, 4)]

    mine = ang_s[yh * 2 + k]
    same = [jnp.where(ang_s[u] == mine, 1.0, 0.0) for u in fours]
    turned = [jnp.where(ang_s[u] == lax.rem(mine + 2, 4), 1.0, 0.0) for u in fours]
    other = [1.0 - same[u] - turned[u] for u in fours]
    members = same[0] + same[1] + same[2] + same[3] + turned[0] + turned[1] + turned[2] + turned[3]
    for comp in range(2):
        rows = slice(32 * comp, 32 * comp + 32)
        line = lines[rows]
        spread = (4.0 - members) * lines[64 + comp : 65 + comp]
        mix = members * line
        for u in fours:
            mix = mix - same[u] * qs[u, rows] - turned[u] * qm[u, rows]
            spread = spread - other[u] * (qs[u, 64 + comp : 65 + comp] + qm[u, 64 + comp : 65 + comp])
        fresh = line - 0.25 * (mix + spread * (1.0 / TOTAL))
        fresh_o[comp] = fresh
        keep = jnp.zeros((32, 128), F32)
        for u in fours:
            keep = keep + jnp.where(yh * 2 + k == u, qs[u, rows], 0.0)
        renew_o[comp] = rho * (keep - fresh)

    @pl.when(swapped)
    def _():
        for i, (src, _, dst) in enumerate(trades):
            drain(dst, sem_swap_send.at[i])
        drain(qmsg, sem_q_s.at[2])

    drain(qs, sem_q_s.at[0])
    drain(qs.at[pl.ds(0, 3)], sem_q_s.at[1])
    for n, strip in ((0, strip1), (1, strip2)):
        drain(strip.at[0, pl.ds(0, 960)], sem_ag_s.at[n])
        drain(strip.at[0], sem_sh_s.at[n])
        for comp in range(2):
            drain(arrived(n, comp), sem_rs_s.at[n, comp])
        drain((sharein1, sharein2)[n], sem_acc_s.at[n])
    for d in range(3):
        drain(posr, sem_ps_s.at[d])
        drain(posall.at[k, z], sem_ps_s.at[3 + d])
        drain(lbuf.at[0], sem_ln_s.at[0, d])
        drain(nbuf.at[0], sem_ln_s.at[1, d])
    drain(posall.at[0], sem_ps_s.at[6])
    for d in range(7):
        drain(nbuf.at[:, :, 0], sem_ln_s.at[2, d])


def shards(objects, probe, positions, amplitudes, reproj_prev, multipliers, volume, angles, penalty):
    across = lambda a: jnp.transpose(a[0], (0, 2, 1))
    any_, vmem, smem = (pl.BlockSpec(memory_space=m) for m in (pl.ANY, pltpu.VMEM, pltpu.SMEM))
    mats = jnp.asarray(dft_matrices())
    dma = pltpu.SemaphoreType.DMA
    out = jax.ShapeDtypeStruct((2, TILE, ROWS), F32)
    scratch = [
        pltpu.VMEM((2, TOTAL, ROWS), F32),
        pltpu.VMEM((2, TOTAL, ROWS), F32),
        pltpu.VMEM((2, 2, 4, 128, 128), F32),
        pltpu.VMEM((2, 2, 4, 128, 128), F32),
        pltpu.VMEM((SCANS, 2, 384, 128), F32),
        pltpu.VMEM((2, 4, 128, 128), F32),
        pltpu.VMEM((2, 4, 128, 128), F32),
        pltpu.VMEM((2, 4, 4, 32, 128), F32),
        pltpu.VMEM((2, 4, 4, 40, 128), F32),
        pltpu.VMEM((2, 15, 32, 128), F32),
        pltpu.VMEM((2, 15, 40, 128), F32),
        pltpu.VMEM((SCANS, 128, 128), F32),
        pltpu.VMEM((SCANS // 2, 128, 256), F32),
        pltpu.VMEM((2, 128, 128), F32),
        pltpu.VMEM((2, 128, 128), F32),
        pltpu.VMEM((2, TILE, ROWS), F32),
        pltpu.VMEM((2, TILE, ROWS), F32),
        pltpu.VMEM((2, TOTAL, TOTAL), F32),
        pltpu.VMEM((2, 2, 256, 256), BF16),
        pltpu.VMEM((SCANS, 128), jnp.int32),
        pltpu.VMEM((SCANS, 128), jnp.int32),
        pltpu.VMEM((2, 4, 4, SCANS, 128), jnp.int32),
        pltpu.SMEM((SCANS, 128), jnp.int32),
        pltpu.VMEM((4, 8, 128), F32),
        pltpu.VMEM((4, 8, 128), F32),
        pltpu.VMEM((4, 4, 8, 1, 128), F32),
        pltpu.VMEM((4, 4, 8, 1, 128), F32),
        pltpu.VMEM((4, 4, 8, 1, 128), F32),
        pltpu.VMEM((4, 4, 2, 4, 1, 128), F32),
        pltpu.VMEM((128, 128), F32),
        pltpu.VMEM((8, 128, 128), F32),
        pltpu.VMEM((8, 128), F32),
        pltpu.VMEM((72, 128), F32),
        pltpu.VMEM((72, 128), F32),
        pltpu.VMEM((8, 72, 128), F32),
        dma((5,)), dma((5,)), dma((2,)), dma((8,)),
        dma((2,)), dma((2, 2, 15)), dma((2,)), dma((2,)),
        dma((2,)), dma((2, 2)), dma((2, 2)), dma((2, 2)),
        dma((3, 8)), dma((3, 8)), dma((8,)), dma((8,)),
        dma((3,)), dma, dma,
    ]
    fresh, renewed = pl.pallas_call(
        kernel,
        out_shape=(pltpu.VMEM((2, TILE, ROWS), F32), pltpu.VMEM((2, TILE, ROWS), F32)),
        in_specs=[smem, smem, smem] + [any_] * 7,
        out_specs=(vmem, vmem),
        scratch_shapes=scratch,
        compiler_params=pltpu.CompilerParams(
            collective_id=0, has_side_effects=True, vmem_limit_bytes=60 * 1024 * 1024
        ),
    )(
        positions,
        angles,
        penalty,
        across(objects),
        probe,
        amplitudes[0],
        across(reproj_prev),
        across(multipliers),
        volume[:, 0],
        mats,
    )
    back = lambda a: jnp.transpose(a, (0, 2, 1))[None]
    return back(fresh), back(renewed)


def solution(mesh):
    return jax.shard_map(
        shards,
        mesh=mesh,
        in_specs=(
            P("view", None, None, "tile"),
            P(),
            P("view", "tile"),
            P("view", "tile", None, None),
            P("view", None, None, "tile"),
            P("view", None, None, "tile"),
            P(None, ("view", "tile"), None, None),
            P(),
            P(),
        ),
        out_specs=(P("view", None, None, "tile"), P("view", None, None, "tile")),
        check_vma=False,
    )
```

```python
import math

import jax
import jax.numpy as jnp
import ml_dtypes
import numpy as np
from jax import lax
from jax.experimental import pallas as pl
from jax.experimental.pallas import tpu as pltpu
from jax.sharding import PartitionSpec as P

ITERS = 2
F32 = jnp.float32
BF16 = jnp.bfloat16
MESH = pl.DeviceIdType.MESH

ROWS = 128
TOTAL = 1024
SCANS = 8
TILE = 32
FLOOR = 0.25 / math.sqrt(SCANS * 32 * ROWS // TOTAL)

PEERS = sorted(
    [(dz, dx) for dz in range(4) for dx in range(4) if (dz, dx) != (0, 0)],
    key=lambda p: -(min(p[0], 4 - p[0]) + min(p[1], 4 - p[1])),
)


def dft_matrices():
    idx = np.arange(ROWS)
    phase = (idx[:, None] * idx[None, :] % ROWS) * (2.0 * math.pi / ROWS)
    c = np.cos(phase) / math.sqrt(ROWS)
    s = -np.sin(phase) / math.sqrt(ROWS)
    out = []
    for m in (np.block([[c, s], [-s, c]]), np.block([[c, -s], [s, c]])):
        m = m.astype(np.float32)
        hi = m.astype(ml_dtypes.bfloat16)
        lo = (m - hi.astype(np.float32)).astype(ml_dtypes.bfloat16)
        out.append(np.stack([hi, lo]))
    return np.stack(out)


def split(x):
    hi = x.astype(BF16)
    return hi, (x - hi.astype(F32)).astype(BF16)


def split3(x):
    hi = x.astype(BF16)
    rest = x - hi.astype(F32)
    mid = rest.astype(BF16)
    return hi, mid, (rest - mid.astype(F32)).astype(BF16)


def dot(a, b):
    return jnp.dot(a, b, preferred_element_type=F32)


def dot_nt(a, b):
    return lax.dot_general(a, b, (((1,), (1,)), ((), ())), preferred_element_type=F32)


def dot_tn(a, b):
    return lax.dot_general(a, b, (((0,), (0,)), ((), ())), preferred_element_type=F32)


def dot3(a, b):
    return dot(a[0], b[0]) + (dot(a[1], b[0]) + dot(a[0], b[1]))


def device(z, y, x, k):
    return ((y // 2) * 2 + k, z * 8 + (y % 2) * 4 + x)


def kernel(
    pos_h, ang_h, pen_h, obj_h, probe_h, amp_h, prev_h, mult_h, vol_h, mat_h,
    fresh_o, renew_o,
    pos_s, ang_s, pen_s, strip1, strip2, acc1, acc2, zbuf, sharein1, sharein2, stage1, stage2, rsin1, rsin2,
    amp_r, amp_t, probe_v, probe_t, prev_r, mult_r, vol_v, mat_v,
    posb, posr, posall, posm, sums, flips, lbuf, mbuf, nbuf, qbuf, qmat, wfull, vec, qmsg, qflip, qall,
    sem_swap, sem_swap_send, sem_loc, sem_vol, sem_ag_s, sem_ag, sem_sh_s, sem_sh, sem_acc_s, sem_acc,
    sem_rs_s, sem_rs, sem_ln_s, sem_ln, sem_ps_s, sem_ps, sem_q_s, sem_q, sem_smem,
):
    view = lax.axis_index("view")
    tile = lax.axis_index("tile")
    yh, k = view // 2, view % 2
    z, yl, x = tile // 8, (tile // 4) % 2, tile % 4
    y = yh * 2 + yl
    role = z * 8 + k * 4 + x
    own = pl.multiple_of(role * TILE, TILE)
    given = pl.multiple_of(tile * TILE, TILE)
    swapped = yl != k
    partner = device(z, yh * 2 + k, x, yl)
    twin = device(z, y, x, 1 - k)
    fours = range(4)

    def local(src, dst, sem):
        return pltpu.make_async_copy(src, dst, sem)

    def remote(src, dst, send, recv, to):
        return pltpu.make_async_remote_copy(
            src_ref=src, dst_ref=dst, send_sem=send, recv_sem=recv, device_id=to, device_id_type=MESH
        )

    def drain(ref, sem):
        pltpu.make_async_copy(ref, ref, sem).wait()

    def peer(dz, dx):
        return device((z + dz) % 4, y, (x + dx) % 4, k)

    barrier = pltpu.get_barrier_semaphore()
    greeted = 0
    for dz, dx in PEERS:
        pl.semaphore_signal(barrier, inc=1, device_id=peer(dz, dx), device_id_type=MESH)
        greeted += 1
    for dy in fours:
        for dk in range(2):
            if (dy, dk) != (0, 0):
                pl.semaphore_signal(
                    barrier, inc=1, device_id=device(z, (y + dy) % 4, x, (k + dk) % 2), device_id_type=MESH
                )
                pl.semaphore_signal(
                    barrier, inc=1, device_id=device(3 - z, (y + dy) % 4, 3 - x, (k + dk) % 2), device_id_type=MESH
                )
                greeted += 2
    loc = [local(probe_h, probe_v, sem_loc.at[0]), local(mat_h, mat_v, sem_loc.at[1])]
    scalars = [
        local(src, dst, sem_loc.at[2 + i])
        for i, (src, dst) in enumerate(((pos_h, pos_s), (ang_h, ang_s), (pen_h, pen_s)))
    ]
    vols = [
        local(vol_h.at[comp], vol_v.at[comp], sem_vol.at[comp])
        for comp in range(2)
    ]
    for copy in scalars + loc + vols:
        copy.start()

    pl.semaphore_wait(barrier, greeted)

    trades = [
        (obj_h, strip1.at[:, pl.ds(given, TILE)], strip1.at[:, pl.ds(own, TILE)]),
        (posb, posr, posr),
        (prev_h, prev_r, prev_r),
        (mult_h, mult_r, mult_r),
        (amp_h, amp_r, amp_r),
    ]

    def start_trade(i):
        src, there, here = trades[i]

        @pl.when(swapped)
        def _():
            remote(src, there, sem_swap_send.at[i], sem_swap.at[i], partner).start()

        @pl.when(jnp.logical_not(swapped))
        def _():
            local(src, here, sem_swap.at[i]).start()

    start_trade(0)
    for copy in scalars:
        copy.wait()
    for p in range(SCANS):
        posb[p : p + 1, :] = jnp.full((1, 128), pos_s[0, p], jnp.int32)
    zeros = jnp.zeros((128, 128), F32)
    for s in range(SCANS):
        for comp in range(2):
            zbuf[s, comp, 0:128] = zeros
            zbuf[s, comp, 256:384] = zeros
    for i in range(1, 4):
        start_trade(i)

    def traded(i):
        drain(trades[i][2], sem_swap.at[i])

    ones8 = jnp.ones((8, 128), BF16)

    def volume_sums(comp):
        col = jnp.zeros((8, 1024), F32)
        vols[comp].wait()
        for q in fours:
            for half in range(2):
                def body(i, carry):
                    col, part = carry
                    base = pl.multiple_of(256 * q + 128 * half + 8 * i, 8)
                    v = vol_v[comp, pl.ds(base, 8), :]
                    r = v[:, 0:128]
                    for j in range(1, 8):
                        r = r + v[:, 128 * j : 128 * j + 128]
                    qmat[pl.ds(pl.multiple_of(8 * i, 8), 8), :] = r
                    return col + v, part

                col, _ = lax.fori_loop(0, 16, body, (col, 0), unroll=4)
                parts = split3(qmat[...])
                line = dot_nt(ones8, parts[0]) + (dot_nt(ones8, parts[1]) + dot_nt(ones8, parts[2]))
                b = 2 * q + half
                sums[2 * comp + 1, b : b + 1, :] = line[0:1]
        for b in range(8):
            sums[2 * comp, b : b + 1, :] = jnp.sum(col[:, 128 * b : 128 * b + 128], axis=0, keepdims=True)

    volume_sums(0)

    def gather_start(strip, n, comp):
        mine = strip.at[comp, pl.ds(own, TILE)]
        for j, (dz, dx) in enumerate(PEERS):
            remote(mine, mine, sem_ag_s.at[n], sem_ag.at[comp, (j + 1) // 2], peer(dz, dx)).start()
        remote(mine, mine, sem_sh_s.at[n], sem_sh.at[n], twin).start()

    def gather_finish(strip, n):
        for comp in range(2):
            for g in reversed(range(8)):
                members = [0] if g == 0 else [2 * g - 1, 2 * g]
                drain(strip.at[comp, pl.ds(0, TILE * len(members))], sem_ag.at[comp, g])
                for j in members:
                    dz, dx = PEERS[j]
                    src = (z - dz + 4) % 4 * 8 + k * 4 + (x - dx + 4) % 4
                    part = strip.at[comp, pl.ds(pl.multiple_of(src * TILE, TILE), TILE)]
                    remote(part, part, sem_sh_s.at[n], sem_sh.at[n], twin).start()
        drain(strip.at[0], sem_sh.at[n])

    traded(0)
    for comp in range(2):
        gather_start(strip1, 0, comp)
    start_trade(4)

    traded(1)
    to_smem = local(posr, posm, sem_smem)
    to_smem.start()
    local(posr, posall.at[k, z, x], sem_ps.at[0]).start()
    for d in range(1, 4):
        remote(posr, posall.at[k, z, x], sem_ps_s.at[0], sem_ps.at[0], peer(0, d)).start()

    volume_sums(1)

    flat = sums[...].reshape(32, 128)
    rr = lax.broadcasted_iota(jnp.int32, (128, 128), 0)
    cc = lax.broadcasted_iota(jnp.int32, (128, 128), 1)
    anti = jnp.where(rr + cc == 127, 1.0, 0.0).astype(BF16)
    parts = split3(flat)
    turned = dot(parts[0], anti) + (dot(parts[1], anti) + dot(parts[2], anti))
    for a in fours:
        for b in range(8):
            flips[a, 7 - b : 8 - b, :] = turned[8 * a + b : 8 * a + b + 1]
    lane = lax.broadcasted_iota(jnp.int32, (8, 128), 1)
    scale = 1.0 / math.sqrt(TOTAL)
    whole = [jnp.sum(jnp.sum(sums[2 * c], axis=1, keepdims=True), axis=0, keepdims=True) * scale for c in range(2)]
    for u in fours:
        angle = ang_s[u]
        lines = []
        for c in range(2):
            lines.append(
                jnp.where(
                    angle == 0,
                    sums[2 * c],
                    jnp.where(angle == 1, sums[2 * c + 1], jnp.where(angle == 2, flips[2 * c], flips[2 * c + 1])),
                )
                * scale
            )
        for j in fours:
            re = lines[0] if j == 0 else pltpu.roll(lines[0], 128 - 32 * j, 1)
            im = lines[1] if j == 1 else pltpu.roll(lines[1], (160 - 32 * j) % 128, 1)
            rows = jnp.where(
                lane < 32,
                re,
                jnp.where(lane < 64, im, jnp.where(lane == 64, whole[0], whole[1])),
            )
            for b in range(8):
                e = (u // 2 * 2 + b % 2) * 2 + u % 2
                lbuf[j, b // 2, e] = rows[b : b + 1]
    local(lbuf.at[x], mbuf.at[x], sem_ln.at[0]).start()
    for d in range(1, 4):
        xd = (x + d) % 4
        remote(lbuf.at[xd], mbuf.at[x], sem_ln_s.at[0], sem_ln.at[0], peer(0, d)).start()

    for copy in loc:
        copy.wait()
    for comp in range(2):
        probe_t[comp] = probe_v[comp].T
    to_smem.wait()

    gather_finish(strip1, 0)

    drain(posall.at[k, z], sem_ps.at[0])
    for d in range(1, 4):
        remote(posall.at[k, z], posall.at[k, z], sem_ps_s.at[1], sem_ps.at[1], peer(d, 0)).start()

    pr, pi = probe_t[0], probe_t[1]

    traded(4)
    for s in range(SCANS):
        amp_t[s // 2, :, (s % 2) * 128 : (s % 2) * 128 + 128] = amp_r[s].T

    def compute(strip):
        pr, pi = probe_t[0], probe_t[1]

        def right_apply(parts, m):
            out = []
            for u in parts:
                hi, lo = split(u)
                both = dot(jnp.concatenate([hi, lo], axis=0), mat_v[m, 0])
                out.append(both[:256] + (both[256:] + dot(hi, mat_v[m, 1])))
            return out

        def left_apply(m, v):
            hi, lo = split(v)
            both = dot(jnp.concatenate([mat_v[m, 0], mat_v[m, 1]], axis=0), hi)
            return both[:256] + (both[256:] + dot(mat_v[m, 0], lo))

        def exits(p):
            out = []
            for i in range(2):
                start = posm[2 * p + i, 0]
                wr = strip[0, pl.ds(start, 128), :]
                wi = strip[1, pl.ds(start, 128), :]
                out.append(jnp.concatenate([pr * wr - pi * wi, pr * wi + pi * wr], axis=1))
            return jnp.concatenate(out, axis=0)

        def turn(v):
            return jnp.concatenate(
                [
                    jnp.concatenate([v[:128, :128], v[128:, :128]], axis=1),
                    jnp.concatenate([v[:128, 128:], v[128:, 128:]], axis=1),
                ],
                axis=0,
            )

        def constrain(p, f):
            fr, fi = f[:128], f[128:]
            g = amp_t[p] * lax.rsqrt(jnp.maximum(fr * fr + fi * fi, FLOOR * FLOOR))
            return jnp.concatenate([fr * g, fi * g], axis=0)

        def keep(p, v):
            for i in range(2):
                br, bi = v[128 * i : 128 * i + 128, :128], v[128 * i : 128 * i + 128, 128:]
                zbuf[2 * p + i, 0, 128:256] = pr * br + pi * bi
                zbuf[2 * p + i, 1, 128:256] = pr * bi - pi * br

        for first in range(0, SCANS // 2, 4):
            group = range(first, first + 4)
            v = [exits(p) for p in group]
            v = right_apply(v, 0)
            v = [left_apply(1, turn(u)) for u in v]
            v = [constrain(p, u) for p, u in zip(group, v)]
            v = [left_apply(0, u) for u in v]
            v = right_apply([turn(u) for u in v], 1)
            for p, u in zip(group, v):
                keep(p, u)

    def own_weight():
        return wfull[role // 4, pl.ds(pl.multiple_of(role % 4 * 32, 32), 32), :]

    def block_sum(comp, b):
        total = None
        for s in range(SCANS):
            off = jnp.clip(128 + 128 * b - posm[s, 0], 0, 256)
            part = zbuf[s, comp, pl.ds(off, 128), :]
            total = part if total is None else total + part
        return total

    def scatter_start(acc, sharein, stage, n, rho):
        if n:
            vec[...] = jnp.zeros((8, 128), F32)
            for comp in range(2):
                extra = mult_r[comp] / rho + (rho * prev_r[comp] - mult_r[comp]) * own_weight()
                vec[comp : comp + 1, :] = jnp.sum(extra, axis=0, keepdims=True)

        def blocks(comp, parity):
            for j in fours:
                i = 2 * j + parity
                total = block_sum(comp, i)
                acc[parity, comp, j] = total
                if n:
                    vec[comp : comp + 1, :] += jnp.sum(total * wfull[i], axis=0, keepdims=True)

        for comp in range(2):
            blocks(comp, 1 - k)
            remote(acc.at[1 - k, comp], sharein.at[comp], sem_acc_s.at[n], sem_acc.at[n, comp], twin).start()
        for comp in range(2):
            blocks(comp, k)
            drain(sharein.at[comp], sem_acc.at[n, comp])
            for zd in fours:
                for xd in fours:
                    rows = slice(32 * xd, 32 * xd + 32)
                    stage[comp, zd, xd, 0:32] = acc[k, comp, zd, rows] + sharein[comp, zd, rows]
                    if n and comp:
                        stage[comp, zd, xd, 32:40] = vec[...]
            mine = pl.ds(0, 32)
            stage[comp, z, x, mine] = stage[comp, z, x, mine] + (rho * prev_r[comp] - mult_r[comp])
            height = 40 if n and comp else 32
            for j, (dz, dx) in enumerate(PEERS):
                remote(
                    stage.at[comp, (z + dz) % 4, (x + dx) % 4, pl.ds(0, height)],
                    scatter_in[n].at[comp, j, pl.ds(0, height)],
                    sem_rs_s.at[n, comp], sem_rs.at[n, comp], peer(dz, dx),
                ).start()

    scatter_in = (rsin1, rsin2)

    def arrived(n, comp):
        return scatter_in[n].at[comp, :, pl.ds(0, 40 if n and comp else 32)]

    def scatter_finish(stage, n, comp):
        drain(arrived(n, comp), sem_rs.at[n, comp])
        height = 40 if n and comp else 32
        total = stage[comp, z, x, 0:height]
        for j in range(15):
            total = total + scatter_in[n][comp, j, 0:height]
        return total

    rho = jnp.full((32, 128), pen_s[0], jnp.int32).astype(F32) / jnp.full((32, 128), pen_s[1], jnp.int32).astype(F32)

    compute(strip1)
    traded(2)
    traded(3)
    scatter_start(acc1, sharein1, stage1, 0, rho)

    drain(posall.at[k, pl.ds(0, 3)], sem_ps.at[1])
    remote(posall.at[k], posall.at[k], sem_ps_s.at[2], sem_ps.at[2], twin).start()
    drain(mbuf, sem_ln.at[0])
    local(mbuf.at[:, z], nbuf.at[z], sem_ln.at[1]).start()
    for d in range(1, 4):
        zd = (z + d) % 4
        remote(mbuf.at[:, zd], nbuf.at[z], sem_ln_s.at[1], sem_ln.at[1], peer(d, 0)).start()

    drain(posall.at[0], sem_ps.at[2])
    where = posall[...].reshape(256, 128)
    lanes = lax.broadcasted_iota(jnp.int32, (256, 128), 1)
    high = jnp.where(lanes == (where >> 7), 1.0, 0.0)
    low = jnp.where(lanes == ((128 - (where & 127)) & 127), 1.0, 0.0)
    counts = dot_tn(high.astype(BF16), low.astype(BF16))
    power = split(pr * pr + pi * pi)
    before = jnp.zeros((128, 128), F32)
    for b in range(8):
        here = pltpu.roll(jnp.broadcast_to(counts[b : b + 1], (128, 128)), 0, 1, stride=1, stride_axis=0)
        toeplitz = jnp.where(rr >= cc, here, before).astype(BF16)
        before = here
        wfull[b] = 1.0 / (dot(toeplitz, power[0]) + dot(toeplitz, power[1]) + rho[0:1])
    weight = own_weight()

    for comp in range(2):
        strip2[comp, pl.ds(own, TILE), :] = scatter_finish(stage1, 0, comp) * weight
        gather_start(strip2, 1, comp)
    drain(nbuf, sem_ln.at[1])
    e = y * 2 + k
    local(nbuf.at[:, :, e], qbuf.at[yh * 2 + k, :, yl], sem_ln.at[2]).start()
    for dy in fours:
        for dk in range(2):
            if (dy, dk) != (0, 0):
                yd, kd = (y + dy) % 4, (k + dk) % 2
                remote(
                    nbuf.at[:, :, yd * 2 + kd], qbuf.at[yh * 2 + k, :, yl],
                    sem_ln_s.at[2], sem_ln.at[2], device(z, yd, x, kd),
                ).start()
    gather_finish(strip2, 1)

    compute(strip2)
    scatter_start(acc2, sharein2, stage2, 1, rho)

    drain(qbuf, sem_ln.at[2])
    for h in range(128):
        qmat[h : h + 1, :] = qbuf[h // 32, h // 8 % 4, h // 4 % 2, h % 4]
    lines = qmat[...].T

    for comp in range(2):
        height = 40 if comp else 32
        total = scatter_finish(stage2, 1, comp)
        qmsg[comp, 0:32] = total[0:32] * weight + mult_r[comp] / rho
        for i in range(32):
            qflip[comp, 31 - i : 32 - i] = qmsg[comp, i : i + 1]
        if comp:
            qmsg[comp, 32:40] = total[32:40]
            qflip[comp, 32:40] = total[32:40]
        part = pl.ds(0, height)
        for u in fours:
            to = device(3 - z, u // 2 * 2 + 1 - k, 3 - x, u % 2)
            remote(qflip.at[comp, part], qall.at[comp, 4 + y, part], sem_q_s.at[comp], sem_q.at[comp], to).start()
        mine = qmsg.at[comp, part], qall.at[comp, y, part]
        for i in range(1, 4):
            to = device(z, ((yh + i // 2) % 2) * 2 + k, x, (k + i % 2) % 2)
            remote(*mine, sem_q_s.at[comp], sem_q.at[comp], to).start()

        @pl.when(swapped)
        def _():
            remote(*mine, sem_q_s.at[comp], sem_q.at[comp], device(z, yh * 2 + k, x, k)).start()

        @pl.when(jnp.logical_not(swapped))
        def _():
            local(*mine, sem_q.at[comp]).start()

    mine = ang_s[yh * 2 + k]
    same = [jnp.where(ang_s[u] == mine, 1.0, 0.0) for u in fours]
    turned = [jnp.where(ang_s[u] == lax.rem(mine + 2, 4), 1.0, 0.0) for u in fours]
    other = [1.0 - same[u] - turned[u] for u in fours]
    members = same[0] + same[1] + same[2] + same[3] + turned[0] + turned[1] + turned[2] + turned[3]
    for comp in range(2):
        drain(qall.at[comp, :, pl.ds(0, 40 if comp else 32)], sem_q.at[comp])
    for comp in range(2):
        line = lines[32 * comp : 32 * comp + 32]
        spread = (4.0 - members) * lines[64 + comp : 65 + comp]
        mix = members * line
        keep = jnp.zeros((32, 128), F32)
        for u in fours:
            here, there = qall[comp, u, 0:32], qall[comp, 4 + u, 0:32]
            mix = mix - same[u] * here - turned[u] * there
            sums_u = qall[1, u, 32 + comp : 33 + comp] + qall[1, 4 + u, 32 + comp : 33 + comp]
            spread = spread - other[u] * sums_u
            keep = keep + jnp.where(yh * 2 + k == u, here, 0.0)
        fresh = line - 0.25 * (mix + spread * (1.0 / TOTAL))
        fresh_o[comp] = fresh
        renew_o[comp] = rho * (keep - fresh)

    @pl.when(swapped)
    def _():
        for i, (src, _, dst) in enumerate(trades):
            drain(dst, sem_swap_send.at[i])
        for comp in range(2):
            drain(qall.at[comp, :, pl.ds(0, 40 if comp else 32)], sem_q_s.at[comp])

    @pl.when(jnp.logical_not(swapped))
    def _():
        for comp in range(2):
            drain(qall.at[comp, pl.ds(0, 7), pl.ds(0, 40 if comp else 32)], sem_q_s.at[comp])

    for n, strip in ((0, strip1), (1, strip2)):
        drain(strip.at[0, pl.ds(0, 960)], sem_ag_s.at[n])
        drain(strip.at[0], sem_sh_s.at[n])
        for comp in range(2):
            drain(arrived(n, comp), sem_rs_s.at[n, comp])
        drain((sharein1, sharein2)[n], sem_acc_s.at[n])
    drain(posall.at[0, 0, pl.ds(0, 3)], sem_ps_s.at[0])
    drain(posall.at[0, pl.ds(0, 3)], sem_ps_s.at[1])
    drain(posall.at[0], sem_ps_s.at[2])
    drain(lbuf.at[pl.ds(0, 3)], sem_ln_s.at[0])
    drain(nbuf.at[pl.ds(0, 3)], sem_ln_s.at[1])
    drain(nbuf.at[:, :, pl.ds(0, 7)], sem_ln_s.at[2])


def shards(objects, probe, positions, amplitudes, reproj_prev, multipliers, volume, angles, penalty):
    across = lambda a: jnp.transpose(a[0], (0, 2, 1))
    any_, vmem = (pl.BlockSpec(memory_space=m) for m in (pl.ANY, pltpu.VMEM))
    mats = jnp.asarray(dft_matrices())
    dma = pltpu.SemaphoreType.DMA
    out = jax.ShapeDtypeStruct((2, TILE, ROWS), F32)
    scratch = [
        pltpu.SMEM((1, SCANS), jnp.int32),
        pltpu.SMEM((4,), jnp.int32),
        pltpu.SMEM((2,), jnp.int32),
        pltpu.VMEM((2, TOTAL, ROWS), F32),
        pltpu.VMEM((2, TOTAL, ROWS), F32),
        pltpu.VMEM((2, 2, 4, 128, 128), F32),
        pltpu.VMEM((2, 2, 4, 128, 128), F32),
        pltpu.VMEM((SCANS, 2, 384, 128), F32),
        pltpu.VMEM((2, 4, 128, 128), F32),
        pltpu.VMEM((2, 4, 128, 128), F32),
        pltpu.VMEM((2, 4, 4, 32, 128), F32),
        pltpu.VMEM((2, 4, 4, 40, 128), F32),
        pltpu.VMEM((2, 15, 32, 128), F32),
        pltpu.VMEM((2, 15, 40, 128), F32),
        pltpu.VMEM((SCANS, 128, 128), F32),
        pltpu.VMEM((SCANS // 2, 128, 256), F32),
        pltpu.VMEM((2, 128, 128), F32),
        pltpu.VMEM((2, 128, 128), F32),
        pltpu.VMEM((2, TILE, ROWS), F32),
        pltpu.VMEM((2, TILE, ROWS), F32),
        pltpu.VMEM((2, TOTAL, TOTAL), F32),
        pltpu.VMEM((2, 2, 256, 256), BF16),
        pltpu.VMEM((SCANS, 128), jnp.int32),
        pltpu.VMEM((SCANS, 128), jnp.int32),
        pltpu.VMEM((2, 4, 4, SCANS, 128), jnp.int32),
        pltpu.SMEM((SCANS, 128), jnp.int32),
        pltpu.VMEM((4, 8, 128), F32),
        pltpu.VMEM((4, 8, 128), F32),
        pltpu.VMEM((4, 4, 8, 1, 128), F32),
        pltpu.VMEM((4, 4, 8, 1, 128), F32),
        pltpu.VMEM((4, 4, 8, 1, 128), F32),
        pltpu.VMEM((4, 4, 2, 4, 1, 128), F32),
        pltpu.VMEM((128, 128), F32),
        pltpu.VMEM((8, 128, 128), F32),
        pltpu.VMEM((8, 128), F32),
        pltpu.VMEM((2, 40, 128), F32),
        pltpu.VMEM((2, 40, 128), F32),
        pltpu.VMEM((2, 8, 40, 128), F32),
        dma((5,)), dma((5,)), dma((5,)), dma((2,)),
        dma((2,)), dma((2, 8)), dma((2,)), dma((2,)),
        dma((2,)), dma((2, 2)), dma((2, 2)), dma((2, 2)),
        dma((3,)), dma((3,)), dma((3,)), dma((3,)),
        dma((2,)), dma((2,)), dma,
    ]
    fresh, renewed = pl.pallas_call(
        kernel,
        out_shape=(pltpu.VMEM((2, TILE, ROWS), F32), pltpu.VMEM((2, TILE, ROWS), F32)),
        in_specs=[any_] * 10,
        out_specs=(vmem, vmem),
        scratch_shapes=scratch,
        compiler_params=pltpu.CompilerParams(
            collective_id=0, has_side_effects=True, vmem_limit_bytes=60 * 1024 * 1024
        ),
    )(
        positions,
        angles,
        penalty,
        across(objects),
        probe,
        amplitudes[0],
        across(reproj_prev),
        across(multipliers),
        volume[:, 0],
        mats,
    )
    back = lambda a: jnp.transpose(a, (0, 2, 1))[None]
    return back(fresh), back(renewed)


def solution(mesh):
    return jax.shard_map(
        shards,
        mesh=mesh,
        in_specs=(
            P("view", None, None, "tile"),
            P(),
            P("view", "tile"),
            P("view", "tile", None, None),
            P("view", None, None, "tile"),
            P("view", None, None, "tile"),
            P(None, ("view", "tile"), None, None),
            P(),
            P(),
        ),
        out_specs=(P("view", None, None, "tile"), P("view", None, None, "tile")),
        check_vma=False,
    )
```

```python
import math

import jax
import jax.numpy as jnp
import ml_dtypes
import numpy as np
from jax import lax
from jax.experimental import pallas as pl
from jax.experimental.pallas import tpu as pltpu
from jax.sharding import PartitionSpec as P

ITERS = 2
F32 = jnp.float32
BF16 = jnp.bfloat16
MESH = pl.DeviceIdType.MESH

ROWS = 128
TOTAL = 1024
SCANS = 8
TILE = 32
FLOOR = 0.25 / math.sqrt(SCANS * 32 * ROWS // TOTAL)

PEERS = sorted(
    [(dz, dx) for dz in range(4) for dx in range(4) if (dz, dx) != (0, 0)],
    key=lambda p: -(min(p[0], 4 - p[0]) + min(p[1], 4 - p[1])),
)


def dft_matrices():
    idx = np.arange(ROWS)
    phase = (idx[:, None] * idx[None, :] % ROWS) * (2.0 * math.pi / ROWS)
    c = np.cos(phase) / math.sqrt(ROWS)
    s = -np.sin(phase) / math.sqrt(ROWS)
    out = []
    for m in (np.block([[c, s], [-s, c]]), np.block([[c, -s], [s, c]])):
        m = m.astype(np.float32)
        hi = m.astype(ml_dtypes.bfloat16)
        lo = (m - hi.astype(np.float32)).astype(ml_dtypes.bfloat16)
        out.append(np.stack([hi, lo]))
    return np.stack(out)


def split(x):
    hi = x.astype(BF16)
    return hi, (x - hi.astype(F32)).astype(BF16)


def split3(x):
    hi = x.astype(BF16)
    rest = x - hi.astype(F32)
    mid = rest.astype(BF16)
    return hi, mid, (rest - mid.astype(F32)).astype(BF16)


def dot(a, b):
    return jnp.dot(a, b, preferred_element_type=F32)


def dot_nt(a, b):
    return lax.dot_general(a, b, (((1,), (1,)), ((), ())), preferred_element_type=F32)


def dot_tn(a, b):
    return lax.dot_general(a, b, (((0,), (0,)), ((), ())), preferred_element_type=F32)


def dot3(a, b):
    return dot(a[0], b[0]) + (dot(a[1], b[0]) + dot(a[0], b[1]))


def device(z, y, x, k):
    return ((y // 2) * 2 + k, z * 8 + (y % 2) * 4 + x)


def kernel(
    pos_h, ang_h, pen_h, obj_h, probe_h, amp_h, prev_h, mult_h, vol_h, mat_h,
    line_o, change_o, renew_o,
    pos_s, ang_s, pen_s, strip1, strip2, acc1, acc2, zbuf, sharein1, sharein2, stage1, stage2, rsin1, rsin2,
    amp_r, amp_t, probe_v, probe_t, prev_r, mult_r, vol_v, mat_v,
    posb, posr, posall, posm, sums, flips, lbuf, mbuf, nbuf, qbuf, qmat, wfull, vec, qmsg, qflip, qall,
    sem_swap, sem_swap_send, sem_loc, sem_vol, sem_ag_s, sem_ag, sem_sh_s, sem_sh, sem_acc_s, sem_acc,
    sem_rs_s, sem_rs, sem_ln_s, sem_ln, sem_ps_s, sem_ps, sem_q_s, sem_q, sem_smem, sem_ring,
):
    view = lax.axis_index("view")
    tile = lax.axis_index("tile")
    yh, k = view // 2, view % 2
    z, yl, x = tile // 8, (tile // 4) % 2, tile % 4
    y = yh * 2 + yl
    role = z * 8 + k * 4 + x
    own = pl.multiple_of(role * TILE, TILE)
    given = pl.multiple_of(tile * TILE, TILE)
    swapped = yl != k
    partner = device(z, yh * 2 + k, x, yl)
    twin = device(z, y, x, 1 - k)
    fours = range(4)

    def local(src, dst, sem):
        return pltpu.make_async_copy(src, dst, sem)

    def remote(src, dst, send, recv, to):
        return pltpu.make_async_remote_copy(
            src_ref=src, dst_ref=dst, send_sem=send, recv_sem=recv, device_id=to, device_id_type=MESH
        )

    def drain(ref, sem):
        pltpu.make_async_copy(ref, ref, sem).wait()

    def peer(dz, dx):
        return device((z + dz) % 4, y, (x + dx) % 4, k)

    barrier = pltpu.get_barrier_semaphore()
    near = [peer(0, d) for d in (2, 1, 3)] + [peer(d, 0) for d in (2, 1, 3)]
    for dy in (2, 1, 3, 0):
        for dk in range(2):
            if (dy, dk) != (0, 0):
                near.append(device(z, (y + dy) % 4, x, (k + dk) % 2))
    for to in near:
        pl.semaphore_signal(barrier, inc=1, device_id=to, device_id_type=MESH)
    loc = [local(probe_h, probe_v, sem_loc.at[0]), local(mat_h, mat_v, sem_loc.at[1])]
    scalars = [
        local(src, dst, sem_loc.at[2 + i])
        for i, (src, dst) in enumerate(((pos_h, pos_s), (ang_h, ang_s), (pen_h, pen_s)))
    ]
    vols = [
        local(vol_h.at[comp], vol_v.at[comp], sem_vol.at[comp])
        for comp in range(2)
    ]
    for copy in scalars + loc + vols:
        copy.start()

    pl.semaphore_wait(barrier, len(near))

    trades = [
        (obj_h, strip1.at[:, pl.ds(given, TILE)], strip1.at[:, pl.ds(own, TILE)]),
        (posb, posr, posr),
        (prev_h, prev_r, prev_r),
        (mult_h, mult_r, mult_r),
        (amp_h, amp_r, amp_r),
    ]

    def start_trade(i):
        src, there, here = trades[i]

        @pl.when(swapped)
        def _():
            remote(src, there, sem_swap_send.at[i], sem_swap.at[i], partner).start()

        @pl.when(jnp.logical_not(swapped))
        def _():
            local(src, here, sem_swap.at[i]).start()

    start_trade(0)
    for d in (2, 1, 3):
        pl.semaphore_signal(sem_ring, inc=1, device_id=peer(0, d), device_id_type=MESH)
    for copy in scalars:
        copy.wait()
    for p in range(SCANS):
        posb[p : p + 1, :] = jnp.full((1, 128), pos_s[0, p], jnp.int32)
    zeros = jnp.zeros((128, 128), F32)
    for s in range(SCANS):
        for comp in range(2):
            zbuf[s, comp, 0:128] = zeros
            zbuf[s, comp, 256:384] = zeros
    for i in range(1, 4):
        start_trade(i)

    def traded(i):
        drain(trades[i][2], sem_swap.at[i])

    ones8 = jnp.ones((8, 128), BF16)

    def volume_sums(comp):
        col = jnp.zeros((8, 1024), F32)
        vols[comp].wait()
        for q in fours:
            for half in range(2):
                def body(i, carry):
                    col, part = carry
                    base = pl.multiple_of(256 * q + 128 * half + 8 * i, 8)
                    v = vol_v[comp, pl.ds(base, 8), :]
                    r = v[:, 0:128]
                    for j in range(1, 8):
                        r = r + v[:, 128 * j : 128 * j + 128]
                    qmat[pl.ds(pl.multiple_of(8 * i, 8), 8), :] = r
                    return col + v, part

                col, _ = lax.fori_loop(0, 16, body, (col, 0), unroll=4)
                parts = split3(qmat[...])
                line = dot_nt(ones8, parts[0]) + (dot_nt(ones8, parts[1]) + dot_nt(ones8, parts[2]))
                b = 2 * q + half
                sums[2 * comp + 1, b : b + 1, :] = line[0:1]
        for b in range(8):
            sums[2 * comp, b : b + 1, :] = jnp.sum(col[:, 128 * b : 128 * b + 128], axis=0, keepdims=True)


    def gather_start(strip, n, comp):
        mine = strip.at[comp, pl.ds(own, TILE)]
        for j, (dz, dx) in enumerate(PEERS):
            remote(mine, mine, sem_ag_s.at[n], sem_ag.at[comp, (j + 1) // 2], peer(dz, dx)).start()
        remote(mine, mine, sem_sh_s.at[n], sem_sh.at[n], twin).start()

    def gather_finish(strip, n):
        for comp in range(2):
            for g in reversed(range(8)):
                members = [0] if g == 0 else [2 * g - 1, 2 * g]
                drain(strip.at[comp, pl.ds(0, TILE * len(members))], sem_ag.at[comp, g])
                for j in members:
                    dz, dx = PEERS[j]
                    src = (z - dz + 4) % 4 * 8 + k * 4 + (x - dx + 4) % 4
                    part = strip.at[comp, pl.ds(pl.multiple_of(src * TILE, TILE), TILE)]
                    remote(part, part, sem_sh_s.at[n], sem_sh.at[n], twin).start()
        drain(strip.at[0], sem_sh.at[n])

    pl.semaphore_wait(sem_ring, 3)
    traded(0)
    for comp in range(2):
        gather_start(strip1, 0, comp)
    start_trade(4)

    traded(1)
    to_smem = local(posr, posm, sem_smem)
    to_smem.start()
    local(posr, posall.at[k, z, x], sem_ps.at[0]).start()
    for d in range(1, 4):
        remote(posr, posall.at[k, z, x], sem_ps_s.at[0], sem_ps.at[0], peer(0, d)).start()

    rr = lax.broadcasted_iota(jnp.int32, (128, 128), 0)
    cc = lax.broadcasted_iota(jnp.int32, (128, 128), 1)
    scale = 1.0 / math.sqrt(TOTAL)
    for copy in loc:
        copy.wait()
    for comp in range(2):
        probe_t[comp] = probe_v[comp].T
    to_smem.wait()

    volume_sums(0)
    gather_finish(strip1, 0)

    drain(posall.at[k, z], sem_ps.at[0])
    for d in range(1, 4):
        remote(posall.at[k, z], posall.at[k, z], sem_ps_s.at[1], sem_ps.at[1], peer(d, 0)).start()

    pr, pi = probe_t[0], probe_t[1]

    traded(4)
    for s in range(SCANS):
        amp_t[s // 2, :, (s % 2) * 128 : (s % 2) * 128 + 128] = amp_r[s].T

    def compute(strip):
        pr, pi = probe_t[0], probe_t[1]

        def right_apply(parts, m):
            out = []
            for u in parts:
                hi, lo = split(u)
                both = dot(jnp.concatenate([hi, lo], axis=0), mat_v[m, 0])
                out.append(both[:256] + (both[256:] + dot(hi, mat_v[m, 1])))
            return out

        def left_apply(m, v):
            hi, lo = split(v)
            both = dot(jnp.concatenate([mat_v[m, 0], mat_v[m, 1]], axis=0), hi)
            return both[:256] + (both[256:] + dot(mat_v[m, 0], lo))

        def exits(p):
            out = []
            for i in range(2):
                start = posm[2 * p + i, 0]
                wr = strip[0, pl.ds(start, 128), :]
                wi = strip[1, pl.ds(start, 128), :]
                out.append(jnp.concatenate([pr * wr - pi * wi, pr * wi + pi * wr], axis=1))
            return jnp.concatenate(out, axis=0)

        def turn(v):
            return jnp.concatenate(
                [
                    jnp.concatenate([v[:128, :128], v[128:, :128]], axis=1),
                    jnp.concatenate([v[:128, 128:], v[128:, 128:]], axis=1),
                ],
                axis=0,
            )

        def constrain(p, f):
            fr, fi = f[:128], f[128:]
            g = amp_t[p] * lax.rsqrt(jnp.maximum(fr * fr + fi * fi, FLOOR * FLOOR))
            return jnp.concatenate([fr * g, fi * g], axis=0)

        def keep(p, v):
            for i in range(2):
                br, bi = v[128 * i : 128 * i + 128, :128], v[128 * i : 128 * i + 128, 128:]
                zbuf[2 * p + i, 0, 128:256] = pr * br + pi * bi
                zbuf[2 * p + i, 1, 128:256] = pr * bi - pi * br

        for first in range(0, SCANS // 2, 4):
            group = range(first, first + 4)
            v = [exits(p) for p in group]
            v = right_apply(v, 0)
            v = [left_apply(1, turn(u)) for u in v]
            v = [constrain(p, u) for p, u in zip(group, v)]
            v = [left_apply(0, u) for u in v]
            v = right_apply([turn(u) for u in v], 1)
            for p, u in zip(group, v):
                keep(p, u)

    def own_weight():
        return wfull[role // 4, pl.ds(pl.multiple_of(role % 4 * 32, 32), 32), :]

    def block_sum(comp, b):
        total = None
        for s in range(SCANS):
            off = jnp.clip(128 + 128 * b - posm[s, 0], 0, 256)
            part = zbuf[s, comp, pl.ds(off, 128), :]
            total = part if total is None else total + part
        return total

    def scatter_start(acc, sharein, stage, n, rho):
        if n:
            vec[...] = jnp.zeros((8, 128), F32)
            for comp in range(2):
                extra = mult_r[comp] / rho + (rho * prev_r[comp] - mult_r[comp]) * own_weight()
                vec[comp : comp + 1, :] = jnp.sum(extra, axis=0, keepdims=True)

        def blocks(comp, parity):
            for j in fours:
                i = 2 * j + parity
                total = block_sum(comp, i)
                acc[parity, comp, j] = total
                if n:
                    vec[comp : comp + 1, :] += jnp.sum(total * wfull[i], axis=0, keepdims=True)

        for comp in range(2):
            blocks(comp, 1 - k)
            remote(acc.at[1 - k, comp], sharein.at[comp], sem_acc_s.at[n], sem_acc.at[n, comp], twin).start()
        for comp in range(2):
            blocks(comp, k)
            drain(sharein.at[comp], sem_acc.at[n, comp])
            for zd in fours:
                for xd in fours:
                    rows = slice(32 * xd, 32 * xd + 32)
                    stage[comp, zd, xd, 0:32] = acc[k, comp, zd, rows] + sharein[comp, zd, rows]
                    if n and comp:
                        stage[comp, zd, xd, 32:40] = vec[...]
            mine = pl.ds(0, 32)
            stage[comp, z, x, mine] = stage[comp, z, x, mine] + (rho * prev_r[comp] - mult_r[comp])
            height = 40 if n and comp else 32
            for j, (dz, dx) in enumerate(PEERS):
                remote(
                    stage.at[comp, (z + dz) % 4, (x + dx) % 4, pl.ds(0, height)],
                    scatter_in[n].at[comp, j, pl.ds(0, height)],
                    sem_rs_s.at[n, comp], sem_rs.at[n, comp], peer(dz, dx),
                ).start()

    scatter_in = (rsin1, rsin2)

    def arrived(n, comp):
        return scatter_in[n].at[comp, :, pl.ds(0, 40 if n and comp else 32)]

    def scatter_finish(stage, n, comp):
        drain(arrived(n, comp), sem_rs.at[n, comp])
        height = 40 if n and comp else 32
        total = stage[comp, z, x, 0:height]
        for j in range(15):
            total = total + scatter_in[n][comp, j, 0:height]
        return total

    rho = jnp.full((32, 128), pen_s[0], jnp.int32).astype(F32) / jnp.full((32, 128), pen_s[1], jnp.int32).astype(F32)

    compute(strip1)
    traded(2)
    traded(3)
    scatter_start(acc1, sharein1, stage1, 0, rho)

    drain(posall.at[k, pl.ds(0, 3)], sem_ps.at[1])
    remote(posall.at[k], posall.at[k], sem_ps_s.at[2], sem_ps.at[2], twin).start()
    drain(posall.at[0], sem_ps.at[2])
    where = posall[...].reshape(256, 128)
    lanes = lax.broadcasted_iota(jnp.int32, (256, 128), 1)
    high = jnp.where(lanes == (where >> 7), 1.0, 0.0)
    low = jnp.where(lanes == ((128 - (where & 127)) & 127), 1.0, 0.0)
    counts = dot_tn(high.astype(BF16), low.astype(BF16))
    power = split(pr * pr + pi * pi)
    before = jnp.zeros((128, 128), F32)
    for b in range(8):
        here = pltpu.roll(jnp.broadcast_to(counts[b : b + 1], (128, 128)), 0, 1, stride=1, stride_axis=0)
        toeplitz = jnp.where(rr >= cc, here, before).astype(BF16)
        before = here
        wfull[b] = 1.0 / (dot(toeplitz, power[0]) + dot(toeplitz, power[1]) + rho[0:1])
    weight = own_weight()

    volume_sums(1)

    flat = sums[...].reshape(32, 128)
    anti = jnp.where(rr + cc == 127, 1.0, 0.0).astype(BF16)
    parts = split3(flat)
    turned = dot(parts[0], anti) + (dot(parts[1], anti) + dot(parts[2], anti))
    for a in fours:
        for b in range(8):
            flips[a, 7 - b : 8 - b, :] = turned[8 * a + b : 8 * a + b + 1]
    lane = lax.broadcasted_iota(jnp.int32, (8, 128), 1)
    scale = 1.0 / math.sqrt(TOTAL)
    whole = [jnp.sum(jnp.sum(sums[2 * c], axis=1, keepdims=True), axis=0, keepdims=True) * scale for c in range(2)]
    for u in fours:
        angle = ang_s[u]
        lines = []
        for c in range(2):
            lines.append(
                jnp.where(
                    angle == 0,
                    sums[2 * c],
                    jnp.where(angle == 1, sums[2 * c + 1], jnp.where(angle == 2, flips[2 * c], flips[2 * c + 1])),
                )
                * scale
            )
        for j in fours:
            re = lines[0] if j == 0 else pltpu.roll(lines[0], 128 - 32 * j, 1)
            im = lines[1] if j == 1 else pltpu.roll(lines[1], (160 - 32 * j) % 128, 1)
            rows = jnp.where(
                lane < 32,
                re,
                jnp.where(lane < 64, im, jnp.where(lane == 64, whole[0], whole[1])),
            )
            for b in range(8):
                e = (u // 2 * 2 + b % 2) * 2 + u % 2
                lbuf[j, b // 2, e] = rows[b : b + 1]
    local(lbuf.at[x], mbuf.at[x], sem_ln.at[0]).start()
    for d in range(1, 4):
        xd = (x + d) % 4
        remote(lbuf.at[xd], mbuf.at[x], sem_ln_s.at[0], sem_ln.at[0], peer(0, d)).start()

    for comp in range(2):
        strip2[comp, pl.ds(own, TILE), :] = scatter_finish(stage1, 0, comp) * weight
        gather_start(strip2, 1, comp)
    drain(mbuf, sem_ln.at[0])
    local(mbuf.at[:, z], nbuf.at[z], sem_ln.at[1]).start()
    for d in range(1, 4):
        zd = (z + d) % 4
        remote(mbuf.at[:, zd], nbuf.at[z], sem_ln_s.at[1], sem_ln.at[1], peer(d, 0)).start()

    gather_finish(strip2, 1)

    compute(strip2)
    scatter_start(acc2, sharein2, stage2, 1, rho)

    drain(nbuf, sem_ln.at[1])
    e = y * 2 + k
    local(nbuf.at[:, :, e], qbuf.at[yh * 2 + k, :, yl], sem_ln.at[2]).start()
    for dy in fours:
        for dk in range(2):
            if (dy, dk) != (0, 0):
                yd, kd = (y + dy) % 4, (k + dk) % 2
                remote(
                    nbuf.at[:, :, yd * 2 + kd], qbuf.at[yh * 2 + k, :, yl],
                    sem_ln_s.at[2], sem_ln.at[2], device(z, yd, x, kd),
                ).start()
    for comp in range(2):
        height = 40 if comp else 32
        total = scatter_finish(stage2, 1, comp)
        qmsg[comp, 0:32] = total[0:32] * weight + mult_r[comp] / rho
        for i in range(32):
            qflip[comp, 31 - i : 32 - i] = qmsg[comp, i : i + 1]
        if comp:
            qmsg[comp, 32:40] = total[32:40]
            qflip[comp, 32:40] = total[32:40]
        part = pl.ds(0, height)
        for u in fours:
            to = device(3 - z, u // 2 * 2 + 1 - k, 3 - x, u % 2)
            remote(qflip.at[comp, part], qall.at[comp, 4 + y, part], sem_q_s.at[comp], sem_q.at[comp], to).start()
        mine = qmsg.at[comp, part], qall.at[comp, y, part]
        for i in range(1, 4):
            to = device(z, ((yh + i // 2) % 2) * 2 + k, x, (k + i % 2) % 2)
            remote(*mine, sem_q_s.at[comp], sem_q.at[comp], to).start()

        @pl.when(swapped)
        def _():
            remote(*mine, sem_q_s.at[comp], sem_q.at[comp], device(z, yh * 2 + k, x, k)).start()

        @pl.when(jnp.logical_not(swapped))
        def _():
            local(*mine, sem_q.at[comp]).start()

    drain(qbuf, sem_ln.at[2])
    for h in range(128):
        qmat[h : h + 1, :] = qbuf[h // 32, h // 8 % 4, h // 4 % 2, h % 4]
    lines = qmat[...].T

    mine = ang_s[yh * 2 + k]
    same = [jnp.where(ang_s[u] == mine, 1.0, 0.0) for u in fours]
    turned = [jnp.where(ang_s[u] == lax.rem(mine + 2, 4), 1.0, 0.0) for u in fours]
    other = [1.0 - same[u] - turned[u] for u in fours]
    members = same[0] + same[1] + same[2] + same[3] + turned[0] + turned[1] + turned[2] + turned[3]
    for comp in range(2):
        drain(qall.at[comp, :, pl.ds(0, 40 if comp else 32)], sem_q.at[comp])
    for comp in range(2):
        line = lines[32 * comp : 32 * comp + 32]
        spread = (4.0 - members) * lines[64 + comp : 65 + comp]
        mix = members * line
        keep = jnp.zeros((32, 128), F32)
        for u in fours:
            here, there = qall[comp, u, 0:32], qall[comp, 4 + u, 0:32]
            mix = mix - same[u] * here - turned[u] * there
            sums_u = qall[1, u, 32 + comp : 33 + comp] + qall[1, 4 + u, 32 + comp : 33 + comp]
            spread = spread - other[u] * sums_u
            keep = keep + jnp.where(yh * 2 + k == u, here, 0.0)
        change = 0.25 * (mix + spread * (1.0 / TOTAL))
        line_o[comp] = line
        change_o[comp] = change
        renew_o[comp] = rho * (keep - (line - change)) + change

    @pl.when(swapped)
    def _():
        for i, (src, _, dst) in enumerate(trades):
            drain(dst, sem_swap_send.at[i])
        for comp in range(2):
            drain(qall.at[comp, :, pl.ds(0, 40 if comp else 32)], sem_q_s.at[comp])

    @pl.when(jnp.logical_not(swapped))
    def _():
        for comp in range(2):
            drain(qall.at[comp, pl.ds(0, 7), pl.ds(0, 40 if comp else 32)], sem_q_s.at[comp])

    for n, strip in ((0, strip1), (1, strip2)):
        drain(strip.at[0, pl.ds(0, 960)], sem_ag_s.at[n])
        drain(strip.at[0], sem_sh_s.at[n])
        for comp in range(2):
            drain(arrived(n, comp), sem_rs_s.at[n, comp])
        drain((sharein1, sharein2)[n], sem_acc_s.at[n])
    drain(posall.at[0, 0, pl.ds(0, 3)], sem_ps_s.at[0])
    drain(posall.at[0, pl.ds(0, 3)], sem_ps_s.at[1])
    drain(posall.at[0], sem_ps_s.at[2])
    drain(lbuf.at[pl.ds(0, 3)], sem_ln_s.at[0])
    drain(nbuf.at[pl.ds(0, 3)], sem_ln_s.at[1])
    drain(nbuf.at[:, :, pl.ds(0, 7)], sem_ln_s.at[2])


def shards(objects, probe, positions, amplitudes, reproj_prev, multipliers, volume, angles, penalty):
    across = lambda a: jnp.transpose(a[0], (0, 2, 1))
    any_, vmem = (pl.BlockSpec(memory_space=m) for m in (pl.ANY, pltpu.VMEM))
    mats = jnp.asarray(dft_matrices())
    dma = pltpu.SemaphoreType.DMA
    scratch = [
        pltpu.SMEM((1, SCANS), jnp.int32),
        pltpu.SMEM((4,), jnp.int32),
        pltpu.SMEM((2,), jnp.int32),
        pltpu.VMEM((2, TOTAL, ROWS), F32),
        pltpu.VMEM((2, TOTAL, ROWS), F32),
        pltpu.VMEM((2, 2, 4, 128, 128), F32),
        pltpu.VMEM((2, 2, 4, 128, 128), F32),
        pltpu.VMEM((SCANS, 2, 384, 128), F32),
        pltpu.VMEM((2, 4, 128, 128), F32),
        pltpu.VMEM((2, 4, 128, 128), F32),
        pltpu.VMEM((2, 4, 4, 32, 128), F32),
        pltpu.VMEM((2, 4, 4, 40, 128), F32),
        pltpu.VMEM((2, 15, 32, 128), F32),
        pltpu.VMEM((2, 15, 40, 128), F32),
        pltpu.VMEM((SCANS, 128, 128), F32),
        pltpu.VMEM((SCANS // 2, 128, 256), F32),
        pltpu.VMEM((2, 128, 128), F32),
        pltpu.VMEM((2, 128, 128), F32),
        pltpu.VMEM((2, TILE, ROWS), F32),
        pltpu.VMEM((2, TILE, ROWS), F32),
        pltpu.VMEM((2, TOTAL, TOTAL), F32),
        pltpu.VMEM((2, 2, 256, 256), BF16),
        pltpu.VMEM((SCANS, 128), jnp.int32),
        pltpu.VMEM((SCANS, 128), jnp.int32),
        pltpu.VMEM((2, 4, 4, SCANS, 128), jnp.int32),
        pltpu.SMEM((SCANS, 128), jnp.int32),
        pltpu.VMEM((4, 8, 128), F32),
        pltpu.VMEM((4, 8, 128), F32),
        pltpu.VMEM((4, 4, 8, 1, 128), F32),
        pltpu.VMEM((4, 4, 8, 1, 128), F32),
        pltpu.VMEM((4, 4, 8, 1, 128), F32),
        pltpu.VMEM((4, 4, 2, 4, 1, 128), F32),
        pltpu.VMEM((128, 128), F32),
        pltpu.VMEM((8, 128, 128), F32),
        pltpu.VMEM((8, 128), F32),
        pltpu.VMEM((2, 40, 128), F32),
        pltpu.VMEM((2, 40, 128), F32),
        pltpu.VMEM((2, 8, 40, 128), F32),
        dma((5,)), dma((5,)), dma((5,)), dma((2,)),
        dma((2,)), dma((2, 8)), dma((2,)), dma((2,)),
        dma((2,)), dma((2, 2)), dma((2, 2)), dma((2, 2)),
        dma((3,)), dma((3,)), dma((3,)), dma((3,)),
        dma((2,)), dma((2,)), dma, pltpu.SemaphoreType.REGULAR,
    ]
    line, change, renewed = pl.pallas_call(
        kernel,
        out_shape=(pltpu.VMEM((2, TILE, ROWS), F32),) * 3,
        in_specs=[any_] * 10,
        out_specs=(vmem,) * 3,
        scratch_shapes=scratch,
        compiler_params=pltpu.CompilerParams(
            collective_id=0, has_side_effects=True, vmem_limit_bytes=60 * 1024 * 1024
        ),
    )(
        positions,
        angles,
        penalty,
        across(objects),
        probe,
        amplitudes[0],
        across(reproj_prev),
        across(multipliers),
        volume[:, 0],
        mats,
    )
    back = lambda a: jnp.transpose(a, (0, 2, 1))[None]
    return back(line - change), back(renewed - change)


def solution(mesh):
    return jax.shard_map(
        shards,
        mesh=mesh,
        in_specs=(
            P("view", None, None, "tile"),
            P(),
            P("view", "tile"),
            P("view", "tile", None, None),
            P("view", None, None, "tile"),
            P("view", None, None, "tile"),
            P(None, ("view", "tile"), None, None),
            P(),
            P(),
        ),
        out_specs=(P("view", None, None, "tile"), P("view", None, None, "tile")),
        check_vma=False,
    )
```

```python
import math

import jax
import jax.numpy as jnp
import ml_dtypes
import numpy as np
from jax import lax
from jax.experimental import pallas as pl
from jax.experimental.pallas import tpu as pltpu
from jax.sharding import PartitionSpec as P

ITERS = 2
F32 = jnp.float32
BF16 = jnp.bfloat16
MESH = pl.DeviceIdType.MESH

ROWS = 128
TOTAL = 1024
SCANS = 8
TILE = 32
FLOOR = 0.25 / math.sqrt(SCANS * 32 * ROWS // TOTAL)

PEERS = sorted(
    [(dz, dx) for dz in range(4) for dx in range(4) if (dz, dx) != (0, 0)],
    key=lambda p: -(min(p[0], 4 - p[0]) + min(p[1], 4 - p[1])),
)

GROUP = (0, 0, 1, 1, 1, 2, 2, 2, 3, 3, 3, 4, 4, 4, 4)


def dft_matrices():
    idx = np.arange(ROWS)
    phase = (idx[:, None] * idx[None, :] % ROWS) * (2.0 * math.pi / ROWS)
    c = np.cos(phase) / math.sqrt(ROWS)
    s = -np.sin(phase) / math.sqrt(ROWS)
    out = []
    for m in (np.block([[c, s], [-s, c]]), np.block([[c, -s], [s, c]])):
        m = m.astype(np.float32)
        hi = m.astype(ml_dtypes.bfloat16)
        lo = (m - hi.astype(np.float32)).astype(ml_dtypes.bfloat16)
        out.append(np.stack([hi, lo]))
    return np.stack(out)


def split(x):
    hi = x.astype(BF16)
    return hi, (x - hi.astype(F32)).astype(BF16)


def split3(x):
    hi = x.astype(BF16)
    rest = x - hi.astype(F32)
    mid = rest.astype(BF16)
    return hi, mid, (rest - mid.astype(F32)).astype(BF16)


def dot(a, b):
    return jnp.dot(a, b, preferred_element_type=F32)


def dot_nt(a, b):
    return lax.dot_general(a, b, (((1,), (1,)), ((), ())), preferred_element_type=F32)


def dot_tn(a, b):
    return lax.dot_general(a, b, (((0,), (0,)), ((), ())), preferred_element_type=F32)


def dot3(a, b):
    return dot(a[0], b[0]) + (dot(a[1], b[0]) + dot(a[0], b[1]))


def device(z, y, x, k):
    return ((y // 2) * 2 + k, z * 8 + (y % 2) * 4 + x)


def kernel(
    pos_h, ang_h, pen_h, obj_h, probe_h, amp_h, prev_h, mult_h, vol_h, mat_h,
    line_o, change_o, renew_o,
    pos_s, ang_s, pen_s, strip1, strip2, acc1, acc2, zbuf, sharein1, sharein2, stage1, stage2, rsin1, rsin2,
    amp_r, amp_t, probe_v, probe_t, prev_r, mult_r, vol_v, mat_v,
    posb, posr, posall, posm, sums, flips, lbuf, mbuf, nbuf, qbuf, qmat, wfull, vec, qmsg, qflip, qall,
    sem_swap, sem_swap_send, sem_loc, sem_vol, sem_out, sem_ag, sem_sh, sem_acc,
    sem_rs_s, sem_rs, sem_small_s, sem_ln, sem_ps, sem_q_s, sem_q, sem_smem, sem_ring,
):
    view = lax.axis_index("view")
    tile = lax.axis_index("tile")
    yh, k = view // 2, view % 2
    z, yl, x = tile // 8, (tile // 4) % 2, tile % 4
    y = yh * 2 + yl
    role = z * 8 + k * 4 + x
    own = pl.multiple_of(role * TILE, TILE)
    given = pl.multiple_of(tile * TILE, TILE)
    swapped = yl != k
    partner = device(z, yh * 2 + k, x, yl)
    twin = device(z, y, x, 1 - k)
    fours = range(4)

    def local(src, dst, sem):
        return pltpu.make_async_copy(src, dst, sem)

    def remote(src, dst, send, recv, to):
        return pltpu.make_async_remote_copy(
            src_ref=src, dst_ref=dst, send_sem=send, recv_sem=recv, device_id=to, device_id_type=MESH
        )

    def drain(ref, sem):
        pltpu.make_async_copy(ref, ref, sem).wait()

    def peer(dz, dx):
        return device((z + dz) % 4, y, (x + dx) % 4, k)

    barrier = pltpu.get_barrier_semaphore()
    near = [peer(0, d) for d in (2, 1, 3)] + [peer(d, 0) for d in (2, 1, 3)]
    for dy in (2, 1, 3, 0):
        for dk in range(2):
            if (dy, dk) != (0, 0):
                near.append(device(z, (y + dy) % 4, x, (k + dk) % 2))
    for to in near:
        pl.semaphore_signal(barrier, inc=1, device_id=to, device_id_type=MESH)
    loc = [local(probe_h, probe_v, sem_loc.at[3]), local(mat_h, mat_v, sem_loc.at[3])]
    scalars = [
        local(src, dst, sem_loc.at[i])
        for i, (src, dst) in enumerate(((pos_h, pos_s), (ang_h, ang_s), (pen_h, pen_s)))
    ]
    vols = [
        local(vol_h.at[comp], vol_v.at[comp], sem_vol)
        for comp in range(2)
    ]
    for copy in scalars + loc + vols:
        copy.start()

    pl.semaphore_wait(barrier, len(near))

    trades = [
        (obj_h, strip1.at[:, pl.ds(given, TILE)], strip1.at[:, pl.ds(own, TILE)]),
        (posb, posr, posr),
        (prev_h, prev_r, prev_r),
        (mult_h, mult_r, mult_r),
        (amp_h, amp_r, amp_r),
    ]

    def start_trade(i):
        src, there, here = trades[i]

        @pl.when(swapped)
        def _():
            remote(src, there, sem_swap_send, sem_swap.at[i - i // 3], partner).start()

        @pl.when(jnp.logical_not(swapped))
        def _():
            local(src, here, sem_swap.at[i - i // 3]).start()

    start_trade(0)
    for d in (2, 1, 3):
        pl.semaphore_signal(sem_ring, inc=1, device_id=peer(0, d), device_id_type=MESH)
    for copy in scalars:
        copy.wait()
    for p in range(SCANS):
        posb[p : p + 1, :] = jnp.full((1, 128), pos_s[0, p], jnp.int32)
    posb[SCANS:, :] = jnp.zeros((SCANS, 128), jnp.int32)
    zeros = jnp.zeros((128, 128), F32)
    for s in range(SCANS):
        for comp in range(2):
            zbuf[s, comp, 0:128] = zeros
            zbuf[s, comp, 256:384] = zeros
    for i in range(1, 4):
        start_trade(i)

    def spare(rows):
        return zbuf.at[0, 0, pl.ds(0, rows)] if rows < 384 else strip1.at[:, pl.ds(0, rows // 2)]

    def traded(i, rows):
        drain(spare(rows), sem_swap.at[i])

    ones8 = jnp.ones((8, 128), BF16)

    def volume_sums(comp):
        col = jnp.zeros((8, 1024), F32)
        if comp == 0:
            drain(vol_v, sem_vol)
        for q in fours:
            for half in range(2):
                def body(i, carry):
                    col, part = carry
                    base = pl.multiple_of(256 * q + 128 * half + 8 * i, 8)
                    v = vol_v[comp, pl.ds(base, 8), :]
                    r = v[:, 0:128]
                    for j in range(1, 8):
                        r = r + v[:, 128 * j : 128 * j + 128]
                    qmat[pl.ds(pl.multiple_of(8 * i, 8), 8), :] = r
                    return col + v, part

                col, _ = lax.fori_loop(0, 16, body, (col, 0), unroll=4)
                parts = split3(qmat[...])
                line = dot_nt(ones8, parts[0]) + (dot_nt(ones8, parts[1]) + dot_nt(ones8, parts[2]))
                b = 2 * q + half
                sums[2 * comp + 1, b : b + 1, :] = line[0:1]
        for b in range(8):
            sums[2 * comp, b : b + 1, :] = jnp.sum(col[:, 128 * b : 128 * b + 128], axis=0, keepdims=True)


    def gather_start(strip, n, comp):
        mine = strip.at[comp, pl.ds(own, TILE)]
        for j, (dz, dx) in enumerate(PEERS):
            remote(mine, mine, sem_out, sem_ag.at[comp, GROUP[j]], peer(dz, dx)).start()
        remote(mine, mine, sem_out, sem_sh, twin).start()

    def gather_finish(strip, n):
        for comp in range(2):
            for g in reversed(range(5)):
                members = [j for j in range(15) if GROUP[j] == g]
                drain(strip.at[comp, pl.ds(0, TILE * len(members))], sem_ag.at[comp, g])
                for j in members:
                    dz, dx = PEERS[j]
                    src = (z - dz + 4) % 4 * 8 + k * 4 + (x - dx + 4) % 4
                    part = strip.at[comp, pl.ds(pl.multiple_of(src * TILE, TILE), TILE)]
                    remote(part, part, sem_out, sem_sh, twin).start()
        if n == 0:
            traded(3, 1024)
            for s in range(SCANS):
                amp_t[s // 2, :, (s % 2) * 128 : (s % 2) * 128 + 128] = amp_r[s].T
        drain(strip.at[0], sem_sh)

    pl.semaphore_wait(sem_ring, 3)
    traded(0, 64)
    for comp in range(2):
        gather_start(strip1, 0, comp)
    start_trade(4)

    traded(1, 16)
    mine = posr.at[pl.ds(0, SCANS)]
    to_smem = local(mine, posm, sem_smem)
    to_smem.start()
    local(mine, posall.at[k, z, x], sem_ps.at[0]).start()
    for d in range(1, 4):
        remote(mine, posall.at[k, z, x], sem_small_s, sem_ps.at[0], peer(0, d)).start()

    rr = lax.broadcasted_iota(jnp.int32, (128, 128), 0)
    cc = lax.broadcasted_iota(jnp.int32, (128, 128), 1)
    scale = 1.0 / math.sqrt(TOTAL)
    drain(spare(1280), sem_loc.at[3])
    for comp in range(2):
        probe_t[comp] = probe_v[comp].T
    to_smem.wait()

    volume_sums(0)
    gather_finish(strip1, 0)

    drain(posall.at[k, z], sem_ps.at[0])
    for d in range(1, 4):
        remote(posall.at[k, z], posall.at[k, z], sem_small_s, sem_ps.at[1], peer(d, 0)).start()

    pr, pi = probe_t[0], probe_t[1]


    def compute(strip):
        pr, pi = probe_t[0], probe_t[1]

        def right_apply(parts, m):
            out = []
            for u in parts:
                hi, lo = split(u)
                both = dot(jnp.concatenate([hi, lo], axis=0), mat_v[m, 0])
                out.append(both[:256] + (both[256:] + dot(hi, mat_v[m, 1])))
            return out

        def left_apply(m, v):
            hi, lo = split(v)
            both = dot(jnp.concatenate([mat_v[m, 0], mat_v[m, 1]], axis=0), hi)
            return both[:256] + (both[256:] + dot(mat_v[m, 0], lo))

        def exits(p):
            out = []
            for i in range(2):
                start = posm[2 * p + i, 0]
                wr = strip[0, pl.ds(start, 128), :]
                wi = strip[1, pl.ds(start, 128), :]
                out.append(jnp.concatenate([pr * wr - pi * wi, pr * wi + pi * wr], axis=1))
            return jnp.concatenate(out, axis=0)

        def turn(v):
            return jnp.concatenate(
                [
                    jnp.concatenate([v[:128, :128], v[128:, :128]], axis=1),
                    jnp.concatenate([v[:128, 128:], v[128:, 128:]], axis=1),
                ],
                axis=0,
            )

        def constrain(p, f):
            fr, fi = f[:128], f[128:]
            g = amp_t[p] * lax.rsqrt(jnp.maximum(fr * fr + fi * fi, FLOOR * FLOOR))
            return jnp.concatenate([fr * g, fi * g], axis=0)

        def keep(p, v):
            for i in range(2):
                br, bi = v[128 * i : 128 * i + 128, :128], v[128 * i : 128 * i + 128, 128:]
                zbuf[2 * p + i, 0, 128:256] = pr * br + pi * bi
                zbuf[2 * p + i, 1, 128:256] = pr * bi - pi * br

        for first in range(0, SCANS // 2, 4):
            group = range(first, first + 4)
            v = [exits(p) for p in group]
            v = right_apply(v, 0)
            v = [left_apply(1, turn(u)) for u in v]
            v = [constrain(p, u) for p, u in zip(group, v)]
            v = [left_apply(0, u) for u in v]
            v = right_apply([turn(u) for u in v], 1)
            for p, u in zip(group, v):
                keep(p, u)

    def own_weight():
        return wfull[role // 4, pl.ds(pl.multiple_of(role % 4 * 32, 32), 32), :]

    def block_sum(comp, b):
        total = None
        for s in range(SCANS):
            off = jnp.clip(128 + 128 * b - posm[s, 0], 0, 256)
            part = zbuf[s, comp, pl.ds(off, 128), :]
            total = part if total is None else total + part
        return total

    def scatter_start(acc, sharein, stage, n, rho):
        if n:
            vec[...] = jnp.zeros((8, 128), F32)
            for comp in range(2):
                extra = mult_r[comp] / rho + (rho * prev_r[comp] - mult_r[comp]) * own_weight()
                vec[comp : comp + 1, :] = jnp.sum(extra, axis=0, keepdims=True)

        def blocks(comp, parity, part):
            for j in part:
                i = 2 * j + parity
                total = block_sum(comp, i)
                acc[parity, comp, j] = total
                if n:
                    vec[comp : comp + 1, :] += jnp.sum(total * wfull[i], axis=0, keepdims=True)

        for comp in range(2):
            for half in range(2):
                part = pl.ds(2 * half, 2)
                blocks(comp, 1 - k, (2 * half, 2 * half + 1))
                remote(
                    acc.at[1 - k, comp, part], sharein.at[comp, part], sem_out, sem_acc.at[comp], twin
                ).start()
        for comp in range(2):
            blocks(comp, k, fours)
        for comp in range(2):
            drain(sharein.at[comp], sem_acc.at[comp])
            for zd in fours:
                for xd in fours:
                    rows = slice(32 * xd, 32 * xd + 32)
                    stage[comp, zd, xd, 0:32] = acc[k, comp, zd, rows] + sharein[comp, zd, rows]
                    if n and comp:
                        stage[comp, zd, xd, 32:40] = vec[...]
            mine = pl.ds(0, 32)
            stage[comp, z, x, mine] = stage[comp, z, x, mine] + (rho * prev_r[comp] - mult_r[comp])
            height = 40 if n and comp else 32
            for j, (dz, dx) in enumerate(PEERS):
                remote(
                    stage.at[comp, (z + dz) % 4, (x + dx) % 4, pl.ds(0, height)],
                    scatter_in[n].at[comp, j, pl.ds(0, height)],
                    sem_rs_s.at[n], sem_rs.at[comp], peer(dz, dx),
                ).start()

    scatter_in = (rsin1, rsin2)

    def arrived(n, comp):
        return scatter_in[n].at[comp, :, pl.ds(0, 40 if n and comp else 32)]

    def scatter_finish(stage, n, comp):
        drain(arrived(n, comp), sem_rs.at[comp])
        height = 40 if n and comp else 32
        total = stage[comp, z, x, 0:height]
        for j in range(15):
            total = total + scatter_in[n][comp, j, 0:height]
        return total

    rho = jnp.full((32, 128), pen_s[0], jnp.int32).astype(F32) / jnp.full((32, 128), pen_s[1], jnp.int32).astype(F32)

    compute(strip1)
    traded(2, 128)
    scatter_start(acc1, sharein1, stage1, 0, rho)

    drain(posall.at[k, pl.ds(0, 3)], sem_ps.at[1])
    remote(posall.at[k], posall.at[k], sem_small_s, sem_ps.at[2], twin).start()
    drain(posall.at[0], sem_ps.at[2])
    where = posall[...].reshape(256, 128)
    lanes = lax.broadcasted_iota(jnp.int32, (256, 128), 1)
    high = jnp.where(lanes == (where >> 7), 1.0, 0.0)
    low = jnp.where(lanes == ((128 - (where & 127)) & 127), 1.0, 0.0)
    counts = dot_tn(high.astype(BF16), low.astype(BF16))
    power = split(pr * pr + pi * pi)
    before = jnp.zeros((128, 128), F32)
    for b in range(8):
        here = pltpu.roll(jnp.broadcast_to(counts[b : b + 1], (128, 128)), 0, 1, stride=1, stride_axis=0)
        toeplitz = jnp.where(rr >= cc, here, before).astype(BF16)
        before = here
        wfull[b] = 1.0 / (dot(toeplitz, power[0]) + dot(toeplitz, power[1]) + rho[0:1])
    weight = own_weight()

    volume_sums(1)

    flat = sums[...].reshape(32, 128)
    anti = jnp.where(rr + cc == 127, 1.0, 0.0).astype(BF16)
    parts = split3(flat)
    turned = dot(parts[0], anti) + (dot(parts[1], anti) + dot(parts[2], anti))
    for a in fours:
        for b in range(8):
            flips[a, 7 - b : 8 - b, :] = turned[8 * a + b : 8 * a + b + 1]
    lane = lax.broadcasted_iota(jnp.int32, (8, 128), 1)
    scale = 1.0 / math.sqrt(TOTAL)
    whole = [jnp.sum(jnp.sum(sums[2 * c], axis=1, keepdims=True), axis=0, keepdims=True) * scale for c in range(2)]
    for u in fours:
        angle = ang_s[u]
        lines = []
        for c in range(2):
            lines.append(
                jnp.where(
                    angle == 0,
                    sums[2 * c],
                    jnp.where(angle == 1, sums[2 * c + 1], jnp.where(angle == 2, flips[2 * c], flips[2 * c + 1])),
                )
                * scale
            )
        for j in fours:
            re = lines[0] if j == 0 else pltpu.roll(lines[0], 128 - 32 * j, 1)
            im = lines[1] if j == 1 else pltpu.roll(lines[1], (160 - 32 * j) % 128, 1)
            rows = jnp.where(
                lane < 32,
                re,
                jnp.where(lane < 64, im, jnp.where(lane == 64, whole[0], whole[1])),
            )
            for b in range(8):
                e = (u // 2 * 2 + b % 2) * 2 + u % 2
                lbuf[j, b // 2, e] = rows[b : b + 1]
    local(lbuf.at[x], mbuf.at[x], sem_ln.at[0]).start()
    for d in range(1, 4):
        xd = (x + d) % 4
        remote(lbuf.at[xd], mbuf.at[x], sem_small_s, sem_ln.at[0], peer(0, d)).start()

    for comp in range(2):
        strip2[comp, pl.ds(own, TILE), :] = scatter_finish(stage1, 0, comp) * weight
        gather_start(strip2, 1, comp)
    drain(mbuf, sem_ln.at[0])
    local(mbuf.at[:, z], nbuf.at[z], sem_ln.at[1]).start()
    for d in range(1, 4):
        zd = (z + d) % 4
        remote(mbuf.at[:, zd], nbuf.at[z], sem_small_s, sem_ln.at[1], peer(d, 0)).start()

    gather_finish(strip2, 1)

    compute(strip2)
    scatter_start(acc2, sharein2, stage2, 1, rho)

    drain(nbuf, sem_ln.at[1])
    e = y * 2 + k
    local(nbuf.at[:, :, e], qbuf.at[yh * 2 + k, :, yl], sem_ln.at[2]).start()
    for dy in fours:
        for dk in range(2):
            if (dy, dk) != (0, 0):
                yd, kd = (y + dy) % 4, (k + dk) % 2
                remote(
                    nbuf.at[:, :, yd * 2 + kd], qbuf.at[yh * 2 + k, :, yl],
                    sem_small_s, sem_ln.at[2], device(z, yd, x, kd),
                ).start()
    for comp in range(2):
        height = 40 if comp else 32
        total = scatter_finish(stage2, 1, comp)
        qmsg[comp, 0:32] = total[0:32] * weight + mult_r[comp] / rho
        for i in range(32):
            qflip[comp, 31 - i : 32 - i] = qmsg[comp, i : i + 1]
        if comp:
            qmsg[comp, 32:40] = total[32:40]
            qflip[comp, 32:40] = total[32:40]
        part = pl.ds(0, height)
        for u in fours:
            to = device(3 - z, u // 2 * 2 + 1 - k, 3 - x, u % 2)
            remote(qflip.at[comp, part], qall.at[comp, 4 + y, part], sem_q_s, sem_q.at[comp], to).start()
        mine = qmsg.at[comp, part], qall.at[comp, y, part]
        for i in range(1, 4):
            to = device(z, ((yh + i // 2) % 2) * 2 + k, x, (k + i % 2) % 2)
            remote(*mine, sem_q_s, sem_q.at[comp], to).start()

        @pl.when(swapped)
        def _():
            remote(*mine, sem_q_s, sem_q.at[comp], device(z, yh * 2 + k, x, k)).start()

        @pl.when(jnp.logical_not(swapped))
        def _():
            local(*mine, sem_q.at[comp]).start()

    drain(qbuf, sem_ln.at[2])
    for h in range(128):
        qmat[h : h + 1, :] = qbuf[h // 32, h // 8 % 4, h // 4 % 2, h % 4]
    lines = qmat[...].T

    mine = ang_s[yh * 2 + k]
    same = [jnp.where(ang_s[u] == mine, 1.0, 0.0) for u in fours]
    turned = [jnp.where(ang_s[u] == lax.rem(mine + 2, 4), 1.0, 0.0) for u in fours]
    other = [1.0 - same[u] - turned[u] for u in fours]
    members = same[0] + same[1] + same[2] + same[3] + turned[0] + turned[1] + turned[2] + turned[3]
    for comp in range(2):
        drain(qall.at[comp, :, pl.ds(0, 40 if comp else 32)], sem_q.at[comp])
    for comp in range(2):
        line = lines[32 * comp : 32 * comp + 32]
        spread = (4.0 - members) * lines[64 + comp : 65 + comp]
        mix = members * line
        keep = jnp.zeros((32, 128), F32)
        for u in fours:
            here, there = qall[comp, u, 0:32], qall[comp, 4 + u, 0:32]
            mix = mix - same[u] * here - turned[u] * there
            sums_u = qall[1, u, 32 + comp : 33 + comp] + qall[1, 4 + u, 32 + comp : 33 + comp]
            spread = spread - other[u] * sums_u
            keep = keep + jnp.where(yh * 2 + k == u, here, 0.0)
        change = 0.25 * (mix + spread * (1.0 / TOTAL))
        line_o[comp] = line
        change_o[comp] = change
        renew_o[comp] = rho * (keep - (line - change)) + change

    @pl.when(swapped)
    def _():
        drain(spare(1232), sem_swap_send)
        drain(spare(576), sem_q_s)

    @pl.when(jnp.logical_not(swapped))
    def _():
        drain(strip1.at[0, pl.ds(0, 504)], sem_q_s)

    drain(zbuf.at[:, :, pl.ds(0, 376)], sem_out)
    drain(spare(960), sem_rs_s.at[0])
    drain(zbuf.at[pl.ds(0, 3), 0, pl.ds(0, 360)], sem_rs_s.at[1])
    drain(strip1.at[0, pl.ds(0, 552)], sem_small_s)


def shards(objects, probe, positions, amplitudes, reproj_prev, multipliers, volume, angles, penalty):
    across = lambda a: jnp.transpose(a[0], (0, 2, 1))
    any_, vmem = (pl.BlockSpec(memory_space=m) for m in (pl.ANY, pltpu.VMEM))
    mats = jnp.asarray(dft_matrices())
    dma = pltpu.SemaphoreType.DMA
    scratch = [
        pltpu.SMEM((1, SCANS), jnp.int32),
        pltpu.SMEM((4,), jnp.int32),
        pltpu.SMEM((2,), jnp.int32),
        pltpu.VMEM((2, TOTAL, ROWS), F32),
        pltpu.VMEM((2, TOTAL, ROWS), F32),
        pltpu.VMEM((2, 2, 4, 128, 128), F32),
        pltpu.VMEM((2, 2, 4, 128, 128), F32),
        pltpu.VMEM((SCANS, 2, 384, 128), F32),
        pltpu.VMEM((2, 4, 128, 128), F32),
        pltpu.VMEM((2, 4, 128, 128), F32),
        pltpu.VMEM((2, 4, 4, 32, 128), F32),
        pltpu.VMEM((2, 4, 4, 40, 128), F32),
        pltpu.VMEM((2, 15, 32, 128), F32),
        pltpu.VMEM((2, 15, 40, 128), F32),
        pltpu.VMEM((SCANS, 128, 128), F32),
        pltpu.VMEM((SCANS // 2, 128, 256), F32),
        pltpu.VMEM((2, 128, 128), F32),
        pltpu.VMEM((2, 128, 128), F32),
        pltpu.VMEM((2, TILE, ROWS), F32),
        pltpu.VMEM((2, TILE, ROWS), F32),
        pltpu.VMEM((2, TOTAL, TOTAL), F32),
        pltpu.VMEM((2, 2, 256, 256), BF16),
        pltpu.VMEM((2 * SCANS, 128), jnp.int32),
        pltpu.VMEM((2 * SCANS, 128), jnp.int32),
        pltpu.VMEM((2, 4, 4, SCANS, 128), jnp.int32),
        pltpu.SMEM((SCANS, 128), jnp.int32),
        pltpu.VMEM((4, 8, 128), F32),
        pltpu.VMEM((4, 8, 128), F32),
        pltpu.VMEM((4, 4, 8, 1, 128), F32),
        pltpu.VMEM((4, 4, 8, 1, 128), F32),
        pltpu.VMEM((4, 4, 8, 1, 128), F32),
        pltpu.VMEM((4, 4, 2, 4, 1, 128), F32),
        pltpu.VMEM((128, 128), F32),
        pltpu.VMEM((8, 128, 128), F32),
        pltpu.VMEM((8, 128), F32),
        pltpu.VMEM((2, 40, 128), F32),
        pltpu.VMEM((2, 40, 128), F32),
        pltpu.VMEM((2, 8, 40, 128), F32),
        dma((4,)), dma, dma((4,)), dma, dma, dma((2, 5)), dma, dma((2,)),
        dma((2,)), dma((2,)), dma, dma((3,)), dma((3,)), dma, dma((2,)), dma, pltpu.SemaphoreType.REGULAR,
    ]
    line, change, renewed = pl.pallas_call(
        kernel,
        out_shape=(pltpu.VMEM((2, TILE, ROWS), F32),) * 3,
        in_specs=[any_] * 10,
        out_specs=(vmem,) * 3,
        scratch_shapes=scratch,
        compiler_params=pltpu.CompilerParams(
            collective_id=0, has_side_effects=True, vmem_limit_bytes=60 * 1024 * 1024
        ),
    )(
        positions,
        angles,
        penalty,
        across(objects),
        probe,
        amplitudes[0],
        across(reproj_prev),
        across(multipliers),
        volume[:, 0],
        mats,
    )
    back = lambda a: jnp.transpose(a, (0, 2, 1))[None]
    return back(line - change), back(renewed - change)


def solution(mesh):
    return jax.shard_map(
        shards,
        mesh=mesh,
        in_specs=(
            P("view", None, None, "tile"),
            P(),
            P("view", "tile"),
            P("view", "tile", None, None),
            P("view", None, None, "tile"),
            P("view", None, None, "tile"),
            P(None, ("view", "tile"), None, None),
            P(),
            P(),
        ),
        out_specs=(P("view", None, None, "tile"), P("view", None, None, "tile")),
        check_vma=False,
    )
```

```python
import math

import jax
import jax.numpy as jnp
import ml_dtypes
import numpy as np
from jax import lax
from jax.experimental import pallas as pl
from jax.experimental.pallas import tpu as pltpu
from jax.sharding import PartitionSpec as P

ITERS = 2
F32 = jnp.float32
BF16 = jnp.bfloat16
MESH = pl.DeviceIdType.MESH

ROWS = 128
TOTAL = 1024
SCANS = 8
TILE = 32
FLOOR = 0.25 / math.sqrt(SCANS * 32 * ROWS // TOTAL)

PEERS = sorted(
    [(dz, dx) for dz in range(4) for dx in range(4) if (dz, dx) != (0, 0)],
    key=lambda p: -(min(p[0], 4 - p[0]) + min(p[1], 4 - p[1])),
)

GROUP = (0, 0, 1, 1, 1, 2, 2, 2, 3, 3, 3, 4, 4, 4, 4)


def dft_matrices():
    idx = np.arange(ROWS)
    phase = (idx[:, None] * idx[None, :] % ROWS) * (2.0 * math.pi / ROWS)
    c = np.cos(phase) / math.sqrt(ROWS)
    s = -np.sin(phase) / math.sqrt(ROWS)
    out = []
    for m in (np.block([[c, s], [-s, c]]), np.block([[c, -s], [s, c]])):
        m = m.astype(np.float32)
        hi = m.astype(ml_dtypes.bfloat16)
        lo = (m - hi.astype(np.float32)).astype(ml_dtypes.bfloat16)
        out.append(np.stack([hi, lo]))
    return np.stack(out)


def split(x):
    hi = x.astype(BF16)
    return hi, (x - hi.astype(F32)).astype(BF16)


def split3(x):
    hi = x.astype(BF16)
    rest = x - hi.astype(F32)
    mid = rest.astype(BF16)
    return hi, mid, (rest - mid.astype(F32)).astype(BF16)


def dot(a, b):
    return jnp.dot(a, b, preferred_element_type=F32)


def dot_nt(a, b):
    return lax.dot_general(a, b, (((1,), (1,)), ((), ())), preferred_element_type=F32)


def dot_tn(a, b):
    return lax.dot_general(a, b, (((0,), (0,)), ((), ())), preferred_element_type=F32)


def dot3(a, b):
    return dot(a[0], b[0]) + (dot(a[1], b[0]) + dot(a[0], b[1]))


def device(z, y, x, k):
    return ((y // 2) * 2 + k, z * 8 + (y % 2) * 4 + x)


def kernel(
    pos_h, ang_h, pen_h, obj_h, probe_h, amp_h, prev_h, mult_h, vol_h, mat_h,
    line_o, change_o, renew_o,
    pos_s, ang_s, pen_s, strip1, strip2, acc1, acc2, zbuf, sharein1, sharein2, stage1, stage2, rsin1, rsin2,
    amp_r, amp_t, probe_v, probe_t, prev_r, mult_r, vol_v, mat_v,
    posb, posr, posall, posm, sums, flips, lbuf, mbuf, nbuf, qbuf, qmat, wfull, vec, qmsg, qflip, qall,
    sem_swap, sem_swap_send, sem_loc, sem_vol, sem_out, sem_ag, sem_sh, sem_acc,
    sem_rs_s, sem_rs, sem_small_s, sem_ln, sem_ps, sem_q_s, sem_q, sem_smem, sem_ring,
):
    view = lax.axis_index("view")
    tile = lax.axis_index("tile")
    yh, k = view // 2, view % 2
    z, yl, x = tile // 8, (tile // 4) % 2, tile % 4
    y = yh * 2 + yl
    role = z * 8 + k * 4 + x
    own = pl.multiple_of(role * TILE, TILE)
    given = pl.multiple_of(tile * TILE, TILE)
    swapped = yl != k
    partner = device(z, yh * 2 + k, x, yl)
    twin = device(z, y, x, 1 - k)
    fours = range(4)

    def local(src, dst, sem):
        return pltpu.make_async_copy(src, dst, sem)

    def remote(src, dst, send, recv, to):
        return pltpu.make_async_remote_copy(
            src_ref=src, dst_ref=dst, send_sem=send, recv_sem=recv, device_id=to, device_id_type=MESH
        )

    def drain(ref, sem):
        pltpu.make_async_copy(ref, ref, sem).wait()

    def peer(dz, dx):
        return device((z + dz) % 4, y, (x + dx) % 4, k)

    barrier = pltpu.get_barrier_semaphore()
    near = [peer(0, d) for d in (2, 1, 3)] + [peer(d, 0) for d in (2, 1, 3)]
    for dy in (2, 1, 3, 0):
        for dk in range(2):
            if (dy, dk) != (0, 0):
                near.append(device(z, (y + dy) % 4, x, (k + dk) % 2))
    for to in near:
        pl.semaphore_signal(barrier, inc=1, device_id=to, device_id_type=MESH)
    loc = [local(probe_h, probe_v, sem_loc.at[3]), local(mat_h, mat_v, sem_loc.at[3])]
    scalars = [
        local(src, dst, sem_loc.at[i])
        for i, (src, dst) in enumerate(((pos_h, pos_s), (ang_h, ang_s), (pen_h, pen_s)))
    ]
    vols = [
        local(vol_h.at[comp], vol_v.at[comp], sem_vol)
        for comp in range(2)
    ]
    for copy in scalars + loc + vols:
        copy.start()

    pl.semaphore_wait(barrier, len(near))

    trades = [
        (obj_h, strip1.at[:, pl.ds(given, TILE)], strip1.at[:, pl.ds(own, TILE)]),
        (posb, posr, posr),
        (prev_h, prev_r, prev_r),
        (mult_h, mult_r, mult_r),
        (amp_h, amp_r, amp_r),
    ]

    def start_trade(i):
        src, there, here = trades[i]

        @pl.when(swapped)
        def _():
            remote(src, there, sem_swap_send, sem_swap.at[i - i // 3], partner).start()

        @pl.when(jnp.logical_not(swapped))
        def _():
            local(src, here, sem_swap.at[i - i // 3]).start()

    start_trade(0)
    for d in (2, 1, 3):
        pl.semaphore_signal(sem_ring, inc=1, device_id=peer(0, d), device_id_type=MESH)
    for copy in scalars:
        copy.wait()
    for p in range(SCANS):
        posb[p : p + 1, :] = jnp.full((1, 128), pos_s[0, p], jnp.int32)
    posb[SCANS:, :] = jnp.zeros((SCANS, 128), jnp.int32)
    zeros = jnp.zeros((128, 128), F32)
    for s in range(SCANS):
        for comp in range(2):
            zbuf[s, comp, 0:128] = zeros
            zbuf[s, comp, 256:384] = zeros
    for i in range(1, 4):
        start_trade(i)

    def spare(rows):
        return zbuf.at[0, 0, pl.ds(0, rows)] if rows < 384 else strip1.at[:, pl.ds(0, rows // 2)]

    def traded(i, rows):
        drain(spare(rows), sem_swap.at[i])

    ones8 = jnp.ones((8, 128), BF16)

    def volume_sums(comp):
        col = jnp.zeros((8, 1024), F32)
        if comp == 0:
            drain(vol_v, sem_vol)
        for q in fours:
            for half in range(2):
                def body(i, carry):
                    col, part = carry
                    base = pl.multiple_of(256 * q + 128 * half + 8 * i, 8)
                    v = vol_v[comp, pl.ds(base, 8), :]
                    r = v[:, 0:128]
                    for j in range(1, 8):
                        r = r + v[:, 128 * j : 128 * j + 128]
                    qmat[pl.ds(pl.multiple_of(8 * i, 8), 8), :] = r
                    return col + v, part

                col, _ = lax.fori_loop(0, 16, body, (col, 0), unroll=4)
                parts = split3(qmat[...])
                line = dot_nt(ones8, parts[0]) + (dot_nt(ones8, parts[1]) + dot_nt(ones8, parts[2]))
                b = 2 * q + half
                sums[2 * comp + 1, b : b + 1, :] = line[0:1]
        for b in range(8):
            sums[2 * comp, b : b + 1, :] = jnp.sum(col[:, 128 * b : 128 * b + 128], axis=0, keepdims=True)


    def gather_start(strip, n, comp):
        mine = strip.at[comp, pl.ds(own, TILE)]
        for j, (dz, dx) in enumerate(PEERS):
            remote(mine, mine, sem_out, sem_ag.at[comp, GROUP[j]], peer(dz, dx)).start()
        remote(mine, mine, sem_out, sem_sh, twin).start()

    def gather_finish(strip, n):
        for comp in range(2):
            for g in reversed(range(5)):
                members = [j for j in range(15) if GROUP[j] == g]
                drain(strip.at[comp, pl.ds(0, TILE * len(members))], sem_ag.at[comp, g])
                for j in members:
                    dz, dx = PEERS[j]
                    src = (z - dz + 4) % 4 * 8 + k * 4 + (x - dx + 4) % 4
                    part = strip.at[comp, pl.ds(pl.multiple_of(src * TILE, TILE), TILE)]
                    remote(part, part, sem_out, sem_sh, twin).start()
        if n == 0:
            traded(3, 1024)
            for s in range(SCANS):
                amp_t[s // 2, :, (s % 2) * 128 : (s % 2) * 128 + 128] = amp_r[s].T
        drain(strip.at[0], sem_sh)

    pl.semaphore_wait(sem_ring, 3)
    traded(0, 64)
    for comp in range(2):
        gather_start(strip1, 0, comp)
    start_trade(4)

    traded(1, 16)
    mine = posr.at[pl.ds(0, SCANS)]
    to_smem = local(mine, posm, sem_smem)
    to_smem.start()
    local(mine, posall.at[k, z, x], sem_ps.at[0]).start()
    for d in range(1, 4):
        remote(mine, posall.at[k, z, x], sem_small_s, sem_ps.at[0], peer(0, d)).start()

    rr = lax.broadcasted_iota(jnp.int32, (128, 128), 0)
    cc = lax.broadcasted_iota(jnp.int32, (128, 128), 1)
    scale = 1.0 / math.sqrt(TOTAL)
    drain(spare(1280), sem_loc.at[3])
    for comp in range(2):
        probe_t[comp] = probe_v[comp].T
    to_smem.wait()

    volume_sums(0)
    gather_finish(strip1, 0)

    drain(posall.at[k, z], sem_ps.at[0])
    for d in range(1, 4):
        remote(posall.at[k, z], posall.at[k, z], sem_small_s, sem_ps.at[1], peer(d, 0)).start()

    pr, pi = probe_t[0], probe_t[1]


    def compute(strip):
        pr, pi = probe_t[0], probe_t[1]

        def right_apply(parts, m):
            out = []
            for u in parts:
                hi, lo = split(u)
                both = dot(jnp.concatenate([hi, lo], axis=0), mat_v[m, 0])
                out.append(both[:256] + (both[256:] + dot(hi, mat_v[m, 1])))
            return out

        def left_apply(m, v):
            hi, lo = split(v)
            both = dot(jnp.concatenate([mat_v[m, 0], mat_v[m, 1]], axis=0), hi)
            return both[:256] + (both[256:] + dot(mat_v[m, 0], lo))

        def exits(p):
            out = []
            for i in range(2):
                start = posm[2 * p + i, 0]
                wr = strip[0, pl.ds(start, 128), :]
                wi = strip[1, pl.ds(start, 128), :]
                out.append(jnp.concatenate([pr * wr - pi * wi, pr * wi + pi * wr], axis=1))
            return jnp.concatenate(out, axis=0)

        def turn(v):
            return jnp.concatenate(
                [
                    jnp.concatenate([v[:128, :128], v[128:, :128]], axis=1),
                    jnp.concatenate([v[:128, 128:], v[128:, 128:]], axis=1),
                ],
                axis=0,
            )

        def constrain(p, f):
            fr, fi = f[:128], f[128:]
            g = amp_t[p] * lax.rsqrt(jnp.maximum(fr * fr + fi * fi, FLOOR * FLOOR))
            return jnp.concatenate([fr * g, fi * g], axis=0)

        def keep(p, v):
            for i in range(2):
                br, bi = v[128 * i : 128 * i + 128, :128], v[128 * i : 128 * i + 128, 128:]
                zbuf[2 * p + i, 0, 128:256] = pr * br + pi * bi
                zbuf[2 * p + i, 1, 128:256] = pr * bi - pi * br

        for first in range(0, SCANS // 2, 4):
            group = range(first, first + 4)
            v = [exits(p) for p in group]
            v = right_apply(v, 0)
            v = [left_apply(1, turn(u)) for u in v]
            v = [constrain(p, u) for p, u in zip(group, v)]
            v = [left_apply(0, u) for u in v]
            v = right_apply([turn(u) for u in v], 1)
            for p, u in zip(group, v):
                keep(p, u)

    def own_weight():
        return wfull[role // 4, pl.ds(pl.multiple_of(role % 4 * 32, 32), 32), :]

    def block_sum(comp, b):
        total = None
        for s in range(SCANS):
            off = jnp.clip(128 + 128 * b - posm[s, 0], 0, 256)
            part = zbuf[s, comp, pl.ds(off, 128), :]
            total = part if total is None else total + part
        return total

    def scatter_start(acc, sharein, stage, n, rho):
        if n:
            vec[...] = jnp.zeros((8, 128), F32)
            for comp in range(2):
                extra = mult_r[comp] / rho + (rho * prev_r[comp] - mult_r[comp]) * own_weight()
                vec[comp : comp + 1, :] = jnp.sum(extra, axis=0, keepdims=True)

        def blocks(comp, parity, part):
            for j in part:
                i = 2 * j + parity
                total = block_sum(comp, i)
                acc[parity, comp, j] = total

        for comp in range(2):
            for half in range(2):
                part = pl.ds(2 * half, 2)
                blocks(comp, 1 - k, (2 * half, 2 * half + 1))
                remote(
                    acc.at[1 - k, comp, part], sharein.at[comp, part], sem_out, sem_acc.at[comp], twin
                ).start()
        for comp in range(2):
            blocks(comp, k, fours)
        if n:
            for comp in range(2):
                weighted = acc[k, comp, 0] * wfull[k] + acc[1 - k, comp, 0] * wfull[1 - k]
                for j in range(1, 4):
                    weighted += acc[k, comp, j] * wfull[2 * j + k] + acc[1 - k, comp, j] * wfull[2 * j + 1 - k]
                vec[comp : comp + 1, :] += jnp.sum(weighted, axis=0, keepdims=True)
        for comp in range(2):
            drain(sharein.at[comp], sem_acc.at[comp])
            for zd in fours:
                for xd in fours:
                    rows = slice(32 * xd, 32 * xd + 32)
                    stage[comp, zd, xd, 0:32] = acc[k, comp, zd, rows] + sharein[comp, zd, rows]
                    if n and comp:
                        stage[comp, zd, xd, 32:40] = vec[...]
            mine = pl.ds(0, 32)
            stage[comp, z, x, mine] = stage[comp, z, x, mine] + (rho * prev_r[comp] - mult_r[comp])
            height = 40 if n and comp else 32
            for j, (dz, dx) in enumerate(PEERS):
                remote(
                    stage.at[comp, (z + dz) % 4, (x + dx) % 4, pl.ds(0, height)],
                    scatter_in[n].at[comp, j, pl.ds(0, height)],
                    sem_rs_s.at[n], sem_rs.at[comp], peer(dz, dx),
                ).start()

    scatter_in = (rsin1, rsin2)

    def arrived(n, comp):
        return scatter_in[n].at[comp, :, pl.ds(0, 40 if n and comp else 32)]

    def scatter_finish(stage, n, comp):
        drain(arrived(n, comp), sem_rs.at[comp])
        height = 40 if n and comp else 32
        total = stage[comp, z, x, 0:height]
        for j in range(15):
            total = total + scatter_in[n][comp, j, 0:height]
        return total

    rho = jnp.full((32, 128), pen_s[0], jnp.int32).astype(F32) / jnp.full((32, 128), pen_s[1], jnp.int32).astype(F32)

    compute(strip1)
    traded(2, 128)
    scatter_start(acc1, sharein1, stage1, 0, rho)

    drain(posall.at[k, pl.ds(0, 3)], sem_ps.at[1])
    remote(posall.at[k], posall.at[k], sem_small_s, sem_ps.at[2], twin).start()
    drain(posall.at[0], sem_ps.at[2])
    where = posall[...].reshape(256, 128)
    lanes = lax.broadcasted_iota(jnp.int32, (256, 128), 1)
    high = jnp.where(lanes == (where >> 7), 1.0, 0.0)
    low = jnp.where(lanes == ((128 - (where & 127)) & 127), 1.0, 0.0)
    counts = dot_tn(high.astype(BF16), low.astype(BF16))
    power = split(pr * pr + pi * pi)
    before = jnp.zeros((128, 128), F32)
    for b in range(8):
        here = pltpu.roll(jnp.broadcast_to(counts[b : b + 1], (128, 128)), 0, 1, stride=1, stride_axis=0)
        toeplitz = jnp.where(rr >= cc, here, before).astype(BF16)
        before = here
        wfull[b] = 1.0 / (dot(toeplitz, power[0]) + dot(toeplitz, power[1]) + rho[0:1])
    weight = own_weight()

    volume_sums(1)

    flat = sums[...].reshape(32, 128)
    anti = jnp.where(rr + cc == 127, 1.0, 0.0).astype(BF16)
    parts = split3(flat)
    turned = dot(parts[0], anti) + (dot(parts[1], anti) + dot(parts[2], anti))
    for a in fours:
        for b in range(8):
            flips[a, 7 - b : 8 - b, :] = turned[8 * a + b : 8 * a + b + 1]
    lane = lax.broadcasted_iota(jnp.int32, (8, 128), 1)
    scale = 1.0 / math.sqrt(TOTAL)
    whole = [jnp.sum(jnp.sum(sums[2 * c], axis=1, keepdims=True), axis=0, keepdims=True) * scale for c in range(2)]
    for u in fours:
        angle = ang_s[u]
        lines = []
        for c in range(2):
            lines.append(
                jnp.where(
                    angle == 0,
                    sums[2 * c],
                    jnp.where(angle == 1, sums[2 * c + 1], jnp.where(angle == 2, flips[2 * c], flips[2 * c + 1])),
                )
                * scale
            )
        for j in fours:
            re = lines[0] if j == 0 else pltpu.roll(lines[0], 128 - 32 * j, 1)
            im = lines[1] if j == 1 else pltpu.roll(lines[1], (160 - 32 * j) % 128, 1)
            rows = jnp.where(
                lane < 32,
                re,
                jnp.where(lane < 64, im, jnp.where(lane == 64, whole[0], whole[1])),
            )
            for b in range(8):
                e = (u // 2 * 2 + b % 2) * 2 + u % 2
                lbuf[j, b // 2, e] = rows[b : b + 1]
    local(lbuf.at[x], mbuf.at[x], sem_ln.at[0]).start()
    for d in range(1, 4):
        xd = (x + d) % 4
        remote(lbuf.at[xd], mbuf.at[x], sem_small_s, sem_ln.at[0], peer(0, d)).start()

    for comp in range(2):
        strip2[comp, pl.ds(own, TILE), :] = scatter_finish(stage1, 0, comp) * weight
        gather_start(strip2, 1, comp)
    drain(mbuf, sem_ln.at[0])
    local(mbuf.at[:, z], nbuf.at[z], sem_ln.at[1]).start()
    for d in range(1, 4):
        zd = (z + d) % 4
        remote(mbuf.at[:, zd], nbuf.at[z], sem_small_s, sem_ln.at[1], peer(d, 0)).start()

    gather_finish(strip2, 1)

    compute(strip2)
    scatter_start(acc2, sharein2, stage2, 1, rho)

    drain(nbuf, sem_ln.at[1])
    e = y * 2 + k
    local(nbuf.at[:, :, e], qbuf.at[yh * 2 + k, :, yl], sem_ln.at[2]).start()
    for dy in fours:
        for dk in range(2):
            if (dy, dk) != (0, 0):
                yd, kd = (y + dy) % 4, (k + dk) % 2
                remote(
                    nbuf.at[:, :, yd * 2 + kd], qbuf.at[yh * 2 + k, :, yl],
                    sem_small_s, sem_ln.at[2], device(z, yd, x, kd),
                ).start()
    for comp in range(2):
        height = 40 if comp else 32
        total = scatter_finish(stage2, 1, comp)
        qmsg[comp, 0:32] = total[0:32] * weight + mult_r[comp] / rho
        for i in range(32):
            qflip[comp, 31 - i : 32 - i] = qmsg[comp, i : i + 1]
        if comp:
            qmsg[comp, 32:40] = total[32:40]
            qflip[comp, 32:40] = total[32:40]
        part = pl.ds(0, height)
        mine = qmsg.at[comp, part], qall.at[comp, y, part]
        for i in range(1, 4):
            to = device(z, ((yh + i // 2) % 2) * 2 + k, x, (k + i % 2) % 2)
            remote(*mine, sem_q_s, sem_q.at[comp], to).start()

        @pl.when(swapped)
        def _():
            remote(*mine, sem_q_s, sem_q.at[comp], device(z, yh * 2 + k, x, k)).start()

        @pl.when(jnp.logical_not(swapped))
        def _():
            local(*mine, sem_q.at[comp]).start()

        for u in fours:
            to = device(3 - z, u // 2 * 2 + 1 - k, 3 - x, u % 2)
            remote(qflip.at[comp, part], qall.at[comp, 4 + y, part], sem_q_s, sem_q.at[comp], to).start()

    drain(qbuf, sem_ln.at[2])
    for h in range(128):
        qmat[h : h + 1, :] = qbuf[h // 32, h // 8 % 4, h // 4 % 2, h % 4]
    lines = qmat[...].T

    mine = ang_s[yh * 2 + k]
    same = [jnp.where(ang_s[u] == mine, 1.0, 0.0) for u in fours]
    turned = [jnp.where(ang_s[u] == lax.rem(mine + 2, 4), 1.0, 0.0) for u in fours]
    other = [1.0 - same[u] - turned[u] for u in fours]
    members = same[0] + same[1] + same[2] + same[3] + turned[0] + turned[1] + turned[2] + turned[3]
    for comp in range(2):
        drain(qall.at[comp, :, pl.ds(0, 40 if comp else 32)], sem_q.at[comp])
    for comp in range(2):
        line = lines[32 * comp : 32 * comp + 32]
        spread = (4.0 - members) * lines[64 + comp : 65 + comp]
        mix = members * line
        keep = jnp.zeros((32, 128), F32)
        for u in fours:
            here, there = qall[comp, u, 0:32], qall[comp, 4 + u, 0:32]
            mix = mix - same[u] * here - turned[u] * there
            sums_u = qall[1, u, 32 + comp : 33 + comp] + qall[1, 4 + u, 32 + comp : 33 + comp]
            spread = spread - other[u] * sums_u
            keep = keep + jnp.where(yh * 2 + k == u, here, 0.0)
        change = 0.25 * (mix + spread * (1.0 / TOTAL))
        line_o[comp] = line
        change_o[comp] = change
        renew_o[comp] = rho * (keep - (line - change)) + change

    @pl.when(swapped)
    def _():
        drain(spare(1232), sem_swap_send)
        drain(spare(576), sem_q_s)

    @pl.when(jnp.logical_not(swapped))
    def _():
        drain(strip1.at[0, pl.ds(0, 504)], sem_q_s)

    drain(zbuf.at[:, :, pl.ds(0, 376)], sem_out)
    drain(spare(960), sem_rs_s.at[0])
    drain(zbuf.at[pl.ds(0, 3), 0, pl.ds(0, 360)], sem_rs_s.at[1])
    drain(strip1.at[0, pl.ds(0, 552)], sem_small_s)


def shards(objects, probe, positions, amplitudes, reproj_prev, multipliers, volume, angles, penalty):
    across = lambda a: jnp.transpose(a[0], (0, 2, 1))
    any_, vmem = (pl.BlockSpec(memory_space=m) for m in (pl.ANY, pltpu.VMEM))
    mats = jnp.asarray(dft_matrices())
    dma = pltpu.SemaphoreType.DMA
    scratch = [
        pltpu.SMEM((1, SCANS), jnp.int32),
        pltpu.SMEM((4,), jnp.int32),
        pltpu.SMEM((2,), jnp.int32),
        pltpu.VMEM((2, TOTAL, ROWS), F32),
        pltpu.VMEM((2, TOTAL, ROWS), F32),
        pltpu.VMEM((2, 2, 4, 128, 128), F32),
        pltpu.VMEM((2, 2, 4, 128, 128), F32),
        pltpu.VMEM((SCANS, 2, 384, 128), F32),
        pltpu.VMEM((2, 4, 128, 128), F32),
        pltpu.VMEM((2, 4, 128, 128), F32),
        pltpu.VMEM((2, 4, 4, 32, 128), F32),
        pltpu.VMEM((2, 4, 4, 40, 128), F32),
        pltpu.VMEM((2, 15, 32, 128), F32),
        pltpu.VMEM((2, 15, 40, 128), F32),
        pltpu.VMEM((SCANS, 128, 128), F32),
        pltpu.VMEM((SCANS // 2, 128, 256), F32),
        pltpu.VMEM((2, 128, 128), F32),
        pltpu.VMEM((2, 128, 128), F32),
        pltpu.VMEM((2, TILE, ROWS), F32),
        pltpu.VMEM((2, TILE, ROWS), F32),
        pltpu.VMEM((2, TOTAL, TOTAL), F32),
        pltpu.VMEM((2, 2, 256, 256), BF16),
        pltpu.VMEM((2 * SCANS, 128), jnp.int32),
        pltpu.VMEM((2 * SCANS, 128), jnp.int32),
        pltpu.VMEM((2, 4, 4, SCANS, 128), jnp.int32),
        pltpu.SMEM((SCANS, 128), jnp.int32),
        pltpu.VMEM((4, 8, 128), F32),
        pltpu.VMEM((4, 8, 128), F32),
        pltpu.VMEM((4, 4, 8, 1, 128), F32),
        pltpu.VMEM((4, 4, 8, 1, 128), F32),
        pltpu.VMEM((4, 4, 8, 1, 128), F32),
        pltpu.VMEM((4, 4, 2, 4, 1, 128), F32),
        pltpu.VMEM((128, 128), F32),
        pltpu.VMEM((8, 128, 128), F32),
        pltpu.VMEM((8, 128), F32),
        pltpu.VMEM((2, 40, 128), F32),
        pltpu.VMEM((2, 40, 128), F32),
        pltpu.VMEM((2, 8, 40, 128), F32),
        dma((4,)), dma, dma((4,)), dma, dma, dma((2, 5)), dma, dma((2,)),
        dma((2,)), dma((2,)), dma, dma((3,)), dma((3,)), dma, dma((2,)), dma, pltpu.SemaphoreType.REGULAR,
    ]
    line, change, renewed = pl.pallas_call(
        kernel,
        out_shape=(pltpu.VMEM((2, TILE, ROWS), F32),) * 3,
        in_specs=[any_] * 10,
        out_specs=(vmem,) * 3,
        scratch_shapes=scratch,
        compiler_params=pltpu.CompilerParams(
            collective_id=0, has_side_effects=True, vmem_limit_bytes=60 * 1024 * 1024
        ),
    )(
        positions,
        angles,
        penalty,
        across(objects),
        probe,
        amplitudes[0],
        across(reproj_prev),
        across(multipliers),
        volume[:, 0],
        mats,
    )
    back = lambda a: jnp.transpose(a, (0, 2, 1))[None]
    return back(line - change), back(renewed - change)


def solution(mesh):
    return jax.shard_map(
        shards,
        mesh=mesh,
        in_specs=(
            P("view", None, None, "tile"),
            P(),
            P("view", "tile"),
            P("view", "tile", None, None),
            P("view", None, None, "tile"),
            P("view", None, None, "tile"),
            P(None, ("view", "tile"), None, None),
            P(),
            P(),
        ),
        out_specs=(P("view", None, None, "tile"), P("view", None, None, "tile")),
        check_vma=False,
    )
```
